128 devices in a mesh: seq: 64 (over x, z, y), head: 2 (over core).
Axes of the slice: x: 4, y: 4, z: 4, core: 2. Of those that a mesh axis runs over, the one named last changes fastest.
Arguments:
- queries: bfloat16 [65536, 2048], P('seq', 'head'), may hold values from -5 to 5
- lin_keys: bfloat16 [65536, 2048], P('seq', 'head'), may hold values from -6 to 6
- lin_values: bfloat16 [65536, 2048], P('seq', 'head'), may hold values from -6 to 6
- window_keys: bfloat16 [65536, 512], P('seq', 'head'), may hold values from -5 to 5
- window_values: bfloat16 [65536, 512], P('seq', 'head'), may hold values from -6 to 6
- level_index: int32 [17, 65536], P(None, 'seq'), may hold values from 0 to 7
- level_table: float32 [8, 16], P(None, 'head'), may hold values from 0.25 to 2
- seq_lengths: int32 [4], replicated, may hold values from 1 to 32, 64 in all
- gain_linear: float32 [2048], P('head'), may hold values from 0.25 to 1.75
- gain_window: float32 [2048], P('head'), may hold values from 0.25 to 1.75
- w_out: bfloat16 [2048, 2048], P('head'), may hold values from -0.125 to 0.125
Outputs:
- mixed: bfloat16 [65536, 2048], P(('seq', 'head'))
The draws below stay inside these ranges and needn't reach their ends.
Inputs may be any that keep to these rules, and one draw needn't show every extreme that they name: `seq_lengths`: lengths of 4 consecutive sequences in whole shards of 1024 tokens, in order from token 0; they add up to the shards of seq and the longest has exactly half of them.
All inputs are finite; a program needn't handle non-finite values.
Results may differ from the reference program's by a relative error of at most 0.0095.
Values may be sent and summed in bfloat16 or wider, within the bound.
A program may use at most 128 MiB of HBM per device.

```python
import math
import jax
import jax.numpy as jnp
import numpy as np
from jax import lax

DH = 128
HEADS = 16
KV_HEADS = 4
D = 2048
WINDOW = 256
BLOCK = 512
TABLE = 8
SEQS = 4
TOK_DEV = 1024
TOKENS = 65536
LEVELS = 17
N_SEQ = 64
N_HEAD = 2


def drawn_pair(key):
    base_key = jax.random.fold_in(key, 4242)
    key_one, key_two = jax.random.split(base_key, 2)
    queries = jnp.clip(jax.random.normal(key_one, (TOKENS, HEADS * DH), jnp.float32), -5.0, 5.0)
    keys_window = jnp.clip(jax.random.normal(key_two, (TOKENS, KV_HEADS * DH), jnp.float32), -5.0, 5.0)
    return (queries, keys_window)


def draw_queries(key, part):
    return drawn_pair(key)[0].astype(jnp.bfloat16)


def draw_window_keys(key, part):
    return drawn_pair(key)[1].astype(jnp.bfloat16)


def with_ends(result, own_key, smallest, largest):
    dims = result.shape
    spot = [jax.random.randint(jax.random.fold_in(own_key, axis), (), 0, dims[axis]) for axis in range(len(dims))]
    result = result.at[tuple(spot)].set(smallest)
    longest = dims.index(max(dims))
    spot[longest] = (spot[longest] + 1) % dims[longest]
    return result.at[tuple(spot)].set(largest)


def shard_levels(own_key, extent, cuts, low, top_value):
    loudness = 1.0
    for dim, blocks in cuts:
        steps = jax.random.uniform(jax.random.fold_in(jax.random.fold_in(own_key, 6), dim), (blocks,), jnp.float32, low / len(cuts), top_value / len(cuts))
        loudness = loudness * jnp.repeat(jnp.exp(steps), extent[dim] // blocks).reshape((-1,) + (1,) * (len(extent) - 1 - dim))
    return loudness


def split_up(number_of, total, bound, skew):
    loads = [(1 << 20) // math.isqrt(grade ** skew) + 1 for grade in range(2, number_of + 1)]
    rest, given = total - bound - (number_of - 1), [1] * (number_of - 1)
    while rest > 0:
        free = [i for i in range(number_of - 1) if given[i] < bound]
        mass, left = sum([loads[i] for i in free]), rest
        for i in free:
            addition = min(bound - given[i], max(1, left * loads[i] // mass), rest)
            given[i] = given[i] + addition
            rest = rest - addition
    return np.array([bound] + given)


def uneven(key, amount, total, limit, skew):
    if amount == 2:
        one = jax.random.randint(key, (), max(1, total - limit), min(limit, total - 1) + 1)
        return jnp.stack([one, total - one])
    tallies = jnp.asarray(split_up(amount, total, limit, skew), jnp.int32)
    twos = (amount - 1) // 2
    giver, taker = tallies[1:1 + 2 * twos:2], tallies[2:2 + 2 * twos:2]
    margin = jnp.minimum(giver - 1, limit - taker)
    shifted = jax.random.randint(jax.random.fold_in(key, 1), (twos,), 0, 1 << 20) % (margin + 1)
    tallies = tallies.at[1:1 + 2 * twos:2].set(giver - shifted).at[2:2 + 2 * twos:2].set(taker + shifted)
    return tallies[jax.random.permutation(jax.random.fold_in(key, 2), amount)]


def noise(stream_key, extent, deviation, bound, cuts=(), held_as=jnp.bfloat16):
    values = deviation * jax.random.normal(stream_key, extent, jnp.float32)
    if cuts:
        values = values * shard_levels(stream_key, extent, cuts, -0.22, 0.18)
    return jnp.clip(values, -bound, bound).astype(held_as)


def setup_inputs(seed: int = 0) -> dict:
    key_of = jax.random.split(jax.random.key(seed), 12)
    queries = draw_queries(jax.random.fold_in(key_of[11], 71), 0)
    lin_keys = noise(key_of[1], (TOKENS, HEADS * DH), 1.0, 6.0, ((0, 64), (1, 2)))
    lin_values = noise(key_of[2], (TOKENS, HEADS * DH), 1.0, 6.0, ((0, 64), (1, 2)))
    window_keys = draw_window_keys(jax.random.fold_in(key_of[11], 71), 0)
    window_values = noise(key_of[4], (TOKENS, KV_HEADS * DH), 1.0, 6.0, ((0, 64), (1, 2)))
    level_index = with_ends(jax.random.randint(key_of[5], (LEVELS, TOKENS), 0, TABLE), jax.random.fold_in(key_of[5], 1), 0, TABLE - 1).astype(jnp.int32)
    level_table = jnp.clip(jnp.exp(math.log(2.0) - 2.0794415 * jax.random.uniform(key_of[6], (TABLE, HEADS), jnp.float32) ** shard_levels(key_of[6], (TABLE, HEADS), ((1, 2),), -0.2, 0.2)), 0.25, 2.0)
    seq_lengths = uneven(key_of[7], SEQS, N_SEQ, N_SEQ // 2, 0).astype(jnp.int32)
    gain_linear = jnp.clip(1.0 + 0.15 * jax.random.normal(key_of[8], (HEADS * DH,), jnp.float32), 0.25, 1.75)
    gain_window = jnp.clip(1.0 + 0.15 * jax.random.normal(key_of[9], (HEADS * DH,), jnp.float32), 0.25, 1.75)
    w_out = noise(key_of[10], (HEADS * DH, D), (HEADS * DH) ** -0.5, 0.125, ((0, 2),))
    return {"queries": queries, "lin_keys": lin_keys, "lin_values": lin_values, "window_keys": window_keys, "window_values": window_values, "level_index": level_index, "level_table": level_table, "seq_lengths": seq_lengths, "gain_linear": gain_linear, "gain_window": gain_window, "w_out": w_out}


PRECISE = lax.Precision.HIGHEST
EPSILON = 1e-06

def bit_count(values, bit_width):
    running_total = jnp.zeros_like(values)
    for shift_by in range(bit_width):
        running_total = running_total + (values >= 1 << shift_by).astype(values.dtype)
    return running_total

def round_half(values):
    return lax.optimization_barrier(values.astype(jnp.bfloat16)).astype(jnp.float32)

def rms_scale(values, gain_vector):
    mean_square = lax.optimization_barrier(jnp.mean(values * values, axis=-1, keepdims=True))
    return values * lax.rsqrt(mean_square + EPSILON) * gain_vector

def level_weights(level_index, level_table):
    table_rows = jnp.arange(TABLE, dtype=jnp.int32)
    one_hot = (level_index[:, :, None] == table_rows[None, None, :]).astype(jnp.float32)
    level_scale = jnp.exp2(-0.5 * jnp.arange(LEVELS, dtype=jnp.float32))
    weights = jnp.einsum('ltk,kh->lth', one_hot, level_table.astype(jnp.float32), precision=PRECISE)
    return weights * level_scale[:, None, None]

def reference(queries, lin_keys, lin_values, window_keys, window_values, level_index, level_table, seq_lengths, gain_linear, gain_window, w_out):
    block_count = TOKENS // BLOCK
    block_bits = BLOCK.bit_length() - 1
    cross_levels = LEVELS - 1 - block_bits
    members = HEADS // KV_HEADS
    group_width = HEADS * DH // N_HEAD
    weights = level_weights(level_index, level_table)
    seq_ends = jnp.cumsum(seq_lengths)
    shard_ids = jnp.arange(N_SEQ, dtype=jnp.int32)
    shard_seq = lax.optimization_barrier(jnp.sum((shard_ids[:, None] >= seq_ends[None, :]).astype(jnp.int32), axis=1))
    block_seq = shard_seq[jnp.arange(block_count, dtype=jnp.int32) // (TOK_DEV // BLOCK)]
    query_heads = queries.reshape(TOKENS, HEADS, DH)
    key_heads = lin_keys.reshape(TOKENS, HEADS, DH)
    value_heads = lin_values.reshape(TOKENS, HEADS, DH)

    def block_state(pair_blocks):
        return jnp.einsum('shd,she->hde', pair_blocks[0].astype(jnp.float32), pair_blocks[1].astype(jnp.float32), precision=PRECISE)
    states = lax.map(block_state, (key_heads.reshape(block_count, BLOCK, HEADS, DH), value_heads.reshape(block_count, BLOCK, HEADS, DH)))
    offsets = jnp.arange(BLOCK, dtype=jnp.int32)
    level_grid = bit_count(jnp.bitwise_xor(offsets[:, None], offsets[None, :]), block_bits)
    causal = offsets[None, :] <= offsets[:, None]
    padded_keys = jnp.concatenate([jnp.zeros((WINDOW, KV_HEADS, DH), window_keys.dtype), window_keys.reshape(TOKENS, KV_HEADS, DH)], axis=0)
    padded_values = jnp.concatenate([jnp.zeros((WINDOW, KV_HEADS, DH), window_values.dtype), window_values.reshape(TOKENS, KV_HEADS, DH)], axis=0)
    linear_gain = gain_linear.reshape(HEADS, DH)
    window_gain = gain_window.reshape(HEADS, DH)

    def one_block(block_id):
        first_row = block_id * BLOCK
        query_block = lax.dynamic_slice_in_dim(query_heads, first_row, BLOCK, 0).astype(jnp.float32)
        key_block = lax.dynamic_slice_in_dim(key_heads, first_row, BLOCK, 0).astype(jnp.float32)
        value_block = lax.dynamic_slice_in_dim(value_heads, first_row, BLOCK, 0).astype(jnp.float32)
        weight_block = lax.dynamic_slice_in_dim(weights, first_row, BLOCK, 1)
        scores = jnp.einsum('thd,shd->hts', query_block, key_block, precision=PRECISE)
        mixing = jnp.zeros((HEADS, BLOCK, BLOCK), jnp.float32)
        for level_id in range(block_bits + 1):
            mixing = mixing + jnp.where(level_grid == level_id, 1.0, 0.0)[None, :, :] * weight_block[level_id].T[:, :, None]
        mixing = jnp.where(causal[None, :, :], mixing, 0.0)
        near_part = jnp.einsum('hts,shd->thd', round_half(scores * mixing), value_block, precision=PRECISE)
        far_part = jnp.zeros((BLOCK, HEADS, DH), jnp.float32)
        own_seq = block_seq[block_id]
        for bit_number in range(cross_levels):
            group_span = 1 << bit_number
            upper_edge = block_id // group_span * group_span
            lower_edge = jnp.maximum(upper_edge - group_span, 0).astype(jnp.int32)
            group_states = lax.dynamic_slice_in_dim(states, lower_edge, group_span, 0)
            group_seq = lax.dynamic_slice_in_dim(block_seq, lower_edge, group_span, 0)
            keep_mask = (group_seq == own_seq).astype(jnp.float32)
            bucket = jnp.einsum('j,jhde->hde', keep_mask, group_states, precision=PRECISE)
            present = (block_id // group_span % 2).astype(jnp.float32)
            reached = jnp.einsum('thd,hde->the', query_block, bucket, precision=PRECISE)
            far_part = far_part + present * weight_block[block_bits + 1 + bit_number][:, :, None] * reached
        linear_part = rms_scale(near_part + far_part, linear_gain)
        key_window = lax.dynamic_slice_in_dim(padded_keys, first_row, BLOCK + WINDOW, 0).astype(jnp.float32)
        value_window = lax.dynamic_slice_in_dim(padded_values, first_row, BLOCK + WINDOW, 0).astype(jnp.float32)
        key_pos = first_row - WINDOW + jnp.arange(BLOCK + WINDOW, dtype=jnp.int32)
        query_pos = first_row + offsets
        key_seq = shard_seq[jnp.maximum(key_pos, 0) // TOK_DEV]
        query_seq = shard_seq[query_pos // TOK_DEV]
        allowed = (key_pos[None, :] <= query_pos[:, None]) & (key_pos[None, :] > query_pos[:, None] - WINDOW) & (key_pos[None, :] >= 0) & (key_seq[None, :] == query_seq[:, None])
        grouped = query_block.reshape(BLOCK, KV_HEADS, members, DH)
        logits = jnp.einsum('tkgd,skd->kgts', grouped, key_window, precision=PRECISE) * DH ** (-0.5)
        logits = jnp.where(allowed[None, None, :, :], logits, -1e+30)
        row_peak = lax.optimization_barrier(jnp.max(logits, axis=-1, keepdims=True))
        exponents = jnp.exp(logits - row_peak)
        window_weights = round_half(exponents / lax.optimization_barrier(jnp.sum(exponents, axis=-1, keepdims=True)))
        window_raw = jnp.einsum('kgts,skd->tkgd', window_weights, value_window, precision=PRECISE).reshape(BLOCK, HEADS, DH)
        window_part = rms_scale(window_raw, window_gain)
        attended = (linear_part + window_part).astype(jnp.bfloat16).reshape(BLOCK, HEADS * DH)
        mixed_rows = jnp.zeros((BLOCK, D), jnp.float32)
        for member in range(N_HEAD):
            partial_sum = jnp.dot(attended[:, member * group_width:(member + 1) * group_width], w_out[member * group_width:(member + 1) * group_width], preferred_element_type=jnp.float32)
            mixed_rows = mixed_rows + round_half(partial_sum)
        return mixed_rows.astype(jnp.bfloat16)
    output_blocks = lax.map(one_block, jnp.arange(block_count, dtype=jnp.int32))
    return output_blocks.reshape(TOKENS, D)
```

```python
import functools
import math

import jax
import jax.numpy as jnp
from jax import lax
from jax.experimental import pallas as pl
from jax.experimental.pallas import tpu as pltpu
from jax.sharding import PartitionSpec as P

DH = 128
TILE = 256
EPSILON = 1e-06
SCORE_SCALE = DH ** (-0.5) * math.log2(math.e)
F32 = jnp.float32
BF16 = jnp.bfloat16


def nt(a, b):
    return lax.dot_general(a, b, (((1,), (1,)), ((), ())), preferred_element_type=F32)


def nn(a, b):
    return jnp.dot(a, b, preferred_element_type=F32)


def head_weights(index, table_ref, head):
    weights = jnp.zeros(index.shape, F32)
    for row in range(table_ref.shape[0]):
        weights = jnp.where(index == row, table_ref[row, head], weights)
    level = lax.broadcasted_iota(jnp.int32, (index.shape[0], 1), 0).astype(F32)
    return weights * jnp.exp2(-0.5 * level)


def level_pattern(size):
    s = lax.broadcasted_iota(jnp.int32, (size, size), 0)
    t = lax.broadcasted_iota(jnp.int32, (size, size), 1)
    level = jnp.zeros((size, size), jnp.int32)
    differ = s ^ t
    for bit in range(size.bit_length() - 1):
        level = level + (differ >= (1 << bit)).astype(jnp.int32)
    return jnp.where(s <= t, level, -1)


def near_tile(q, k, vt, rows, pattern):
    half = TILE // 2
    left = nt(k[:half], q)
    right = nt(k[half:], q[half:])
    mix_left = jnp.zeros((half, half), F32)
    mix_right = jnp.zeros((half, half), F32)
    for level in range(8):
        row = rows(level)
        hit = pattern == level
        mix_left = jnp.where(hit, row[:, :half], mix_left)
        mix_right = jnp.where(hit, row[:, half:], mix_right)
    top = jnp.concatenate(
        [(left[:, :half] * mix_left).astype(BF16), (left[:, half:] * rows(8)[:, half:]).astype(BF16)], axis=1
    )
    bottom = jnp.concatenate([jnp.zeros((half, half), BF16), (right * mix_right).astype(BF16)], axis=1)
    return nn(vt, jnp.concatenate([top, bottom], axis=0))


def window_tile(q, keys, vt, current, penalty):
    scores = nt(keys, q)
    previous = scores[:TILE]
    if penalty is not None:
        previous = previous + penalty
    folded = jnp.where(current, scores[TILE:], previous)
    peak = jnp.max(folded, axis=0, keepdims=True)
    exps = jnp.exp2((folded - peak) * SCORE_SCALE)
    total = jnp.sum(exps, axis=0, keepdims=True)
    exps = exps.astype(BF16)
    zero = jnp.zeros_like(exps)
    probs = jnp.concatenate([jnp.where(current, zero, exps), jnp.where(current, exps, zero)], axis=0)
    raw = nn(vt, probs)
    inverse = 1.0 / total
    mean_square = jnp.mean(raw * raw, axis=0, keepdims=True) * (inverse * inverse)
    return raw * (inverse * lax.rsqrt(mean_square + EPSILON))


def states_kernel(k_ref, v_ref, tile_ref, shard_ref):
    total = None
    for tile in range(k_ref.shape[0] // TILE):
        span = pl.ds(tile * TILE, TILE)
        state = nn(v_ref[span, :].T, k_ref[span, :])
        tile_ref[0, tile] = state
        total = state if total is None else total + state
    shard_ref[0] = total


def middle_kernel(
    table_ref, opens_ref, q_ref, k_ref, v_ref, wk_ref, wv_ref, index_ref, tile_ref, gain_ref, near_ref, win_ref, far_w_ref
):
    head = pl.program_id(0)
    weights = head_weights(index_ref[...], table_ref, head)
    far_w_ref[0] = weights
    pattern = level_pattern(TILE // 2)
    s = lax.broadcasted_iota(jnp.int32, (TILE, TILE), 0)
    t = lax.broadcasted_iota(jnp.int32, (TILE, TILE), 1)
    current = s <= t
    gain = gain_ref[0].reshape(DH, 1)
    penalty = -1e30 * opens_ref[0].astype(F32)
    for tile in range(q_ref.shape[0] // TILE):
        first = tile * TILE
        span = pl.ds(first, TILE)
        q, k, vt = q_ref[span, :], k_ref[span, :], v_ref[span, :].T

        def rows(level):
            return weights[level : level + 1, first : first + TILE]

        near = near_tile(q, k, vt, rows, pattern)
        if tile % 2:
            near = near + rows(9) * nt(tile_ref[0, tile - 1].astype(BF16), q)
        if tile >= 2:
            near = near + rows(10) * nt((tile_ref[0, 0] + tile_ref[0, 1]).astype(BF16), q)
        near_ref[0, :, span] = near
        wide = pl.ds(first, 2 * TILE)
        win = window_tile(q, wk_ref[wide, :], wv_ref[wide, :].T, current, penalty if tile == 0 else None)
        win_ref[0, :, span] = win * gain


def last_kernel(keep_ref, q_ref, near_ref, win_ref, w_ref, bucket_ref, gain_ref, w_out_ref, out_ref):
    heads, stages = near_ref.shape[0], bucket_ref.shape[0]
    parts = []
    for head in range(heads):
        q = q_ref[:, head * DH : (head + 1) * DH]
        lin = near_ref[head]
        for stage in range(stages):
            row = w_ref[head, 11 + stage : 12 + stage, :] * keep_ref[stage]
            lin = lin + row * nt(bucket_ref[stage, head], q)
        mean_square = jnp.mean(lin * lin, axis=0, keepdims=True)
        lin = lin * lax.rsqrt(mean_square + EPSILON) * gain_ref[head].reshape(DH, 1)
        parts.append((lin + win_ref[head]).astype(BF16).T)
    attended = jnp.concatenate(parts, axis=1)
    out_ref[...] = nn(attended, w_out_ref[...]).astype(BF16)


def shards(
    queries,
    lin_keys,
    lin_values,
    window_keys,
    window_values,
    level_index,
    level_table,
    seq_lengths,
    gain_linear,
    gain_window,
    w_out,
):
    tokens = queries.shape[0]
    heads = level_table.shape[1]
    groups = window_keys.shape[1] // DH
    members = heads // groups
    levels = level_index.shape[0]
    tiles = tokens // TILE
    shard_count = lax.axis_size("seq")
    stages = shard_count.bit_length() - 1
    shard_id = lax.axis_index("seq")
    seq_starts = jnp.cumsum(seq_lengths) - seq_lengths
    seq_begin = jnp.max(jnp.where(seq_starts <= shard_id, seq_starts, 0))
    opens_here = (seq_begin == shard_id).astype(jnp.int32).reshape(1)

    route = [(i, i + 1) for i in range(shard_count - 1)]
    rim_keys, rim_values = lax.ppermute(
        (window_keys[tokens - TILE :], window_values[tokens - TILE :]), "seq", route
    )
    keys_ext = jnp.concatenate([rim_keys, window_keys], axis=0)
    values_ext = jnp.concatenate([rim_values, window_values], axis=0)

    column = lambda h: (0, h)
    tile_states, running = pl.pallas_call(
        states_kernel,
        grid=(heads,),
        in_specs=[pl.BlockSpec((tokens, DH), column)] * 2,
        out_specs=[
            pl.BlockSpec((1, tiles, DH, DH), lambda h: (h, 0, 0, 0)),
            pl.BlockSpec((1, DH, DH), lambda h: (h, 0, 0)),
        ],
        out_shape=[
            jax.ShapeDtypeStruct((heads, tiles, DH, DH), F32),
            jax.ShapeDtypeStruct((heads, DH, DH), F32),
        ],
        cost_estimate=pl.CostEstimate(flops=2 * tokens * DH * DH * heads, bytes_accessed=8 << 20, transcendentals=0),
    )(lin_keys, lin_values)

    near, win, weights = pl.pallas_call(
        middle_kernel,
        grid=(heads,),
        in_specs=[
            pl.BlockSpec(memory_space=pltpu.SMEM),
            pl.BlockSpec(memory_space=pltpu.SMEM),
            pl.BlockSpec((tokens, DH), column),
            pl.BlockSpec((tokens, DH), column),
            pl.BlockSpec((tokens, DH), column),
            pl.BlockSpec((tokens + TILE, DH), lambda h: (0, h // members)),
            pl.BlockSpec((tokens + TILE, DH), lambda h: (0, h // members)),
            pl.BlockSpec((levels, tokens), lambda h: (0, 0)),
            pl.BlockSpec((1, tiles, DH, DH), lambda h: (h, 0, 0, 0)),
            pl.BlockSpec((1, 1, DH), lambda h: (h, 0, 0)),
        ],
        out_specs=[
            pl.BlockSpec((1, DH, tokens), lambda h: (h, 0, 0)),
            pl.BlockSpec((1, DH, tokens), lambda h: (h, 0, 0)),
            pl.BlockSpec((1, levels, tokens), lambda h: (h, 0, 0)),
        ],
        out_shape=[
            jax.ShapeDtypeStruct((heads, DH, tokens), F32),
            jax.ShapeDtypeStruct((heads, DH, tokens), F32),
            jax.ShapeDtypeStruct((heads, levels, tokens), F32),
        ],
        cost_estimate=pl.CostEstimate(flops=4 << 30, bytes_accessed=20 << 20, transcendentals=4 << 20),
    )(
        level_table,
        opens_here,
        queries,
        lin_keys,
        lin_values,
        keys_ext,
        values_ext,
        level_index,
        tile_states,
        gain_window.reshape(heads, 1, DH),
    )

    buckets, keeps = [], []
    for stage in range(stages):
        span = 1 << stage
        mask = span | (span >> 1 if stage % 2 else 0)
        partner = lax.ppermute(running.astype(BF16), "seq", [(i, i ^ mask) for i in range(shard_count)])
        buckets.append(partner)
        base = shard_id // span * span
        upper = (shard_id // span) % 2 == 1
        other = jnp.where(upper, base - span, base + span)
        opened = jnp.any((seq_starts >= base) & (seq_starts < base + span))
        partner_opened = jnp.any((seq_starts >= other) & (seq_starts < other + span))
        keeps.append((upper & (seq_begin < base)).astype(F32))
        own_scale = jnp.where(upper | jnp.logical_not(partner_opened), 1.0, 0.0)
        partner_scale = jnp.where(upper & opened, 0.0, 1.0)
        running = own_scale * running + partner_scale * partner.astype(F32)

    rows = 256
    partial = pl.pallas_call(
        last_kernel,
        grid=(tokens // rows,),
        in_specs=[
            pl.BlockSpec(memory_space=pltpu.SMEM),
            pl.BlockSpec((rows, heads * DH), lambda i: (i, 0)),
            pl.BlockSpec((heads, DH, rows), lambda i: (0, 0, i)),
            pl.BlockSpec((heads, DH, rows), lambda i: (0, 0, i)),
            pl.BlockSpec((heads, levels, rows), lambda i: (0, 0, i)),
            pl.BlockSpec((stages, heads, DH, DH), lambda i: (0, 0, 0, 0)),
            pl.BlockSpec((heads, 1, DH), lambda i: (0, 0, 0)),
            pl.BlockSpec((heads * DH, w_out.shape[1]), lambda i: (0, 0)),
        ],
        out_specs=pl.BlockSpec((rows, w_out.shape[1]), lambda i: (i, 0)),
        out_shape=jax.ShapeDtypeStruct((tokens, w_out.shape[1]), BF16),
        compiler_params=pltpu.CompilerParams(vmem_limit_bytes=48 << 20),
        cost_estimate=pl.CostEstimate(flops=8 << 30, bytes_accessed=20 << 20, transcendentals=0),
    )(
        jnp.stack(keeps),
        queries,
        near,
        win,
        weights,
        jnp.stack(buckets),
        gain_linear.reshape(heads, 1, DH),
        w_out,
    )
    return lax.psum_scatter(partial, "head", scatter_dimension=0, tiled=True)


def solution(mesh):
    placed = (
        P("seq", "head"),
        P("seq", "head"),
        P("seq", "head"),
        P("seq", "head"),
        P("seq", "head"),
        P(None, "seq"),
        P(None, "head"),
        P(),
        P("head"),
        P("head"),
        P("head", None),
    )
    return jax.shard_map(
        shards, mesh=mesh, in_specs=placed, out_specs=P(("seq", "head"), None), check_vma=False
    )
```

```python
import math

import jax
import jax.numpy as jnp
from jax import lax
from jax.experimental import pallas as pl
from jax.experimental.pallas import tpu as pltpu
from jax.sharding import PartitionSpec as P

DH = 128
TILE = 256
EPSILON = 1e-06
SCORE_SCALE = DH ** (-0.5) * math.log2(math.e)
F32 = jnp.float32
BF16 = jnp.bfloat16
MESH = pl.DeviceIdType.MESH
LAG = 2


def nt(a, b):
    return lax.dot_general(a, b, (((1,), (1,)), ((), ())), preferred_element_type=F32)


def nn(a, b):
    return jnp.dot(a, b, preferred_element_type=F32)


def head_weights(index, table_ref, head):
    weights = jnp.zeros(index.shape, F32)
    for row in range(table_ref.shape[0]):
        weights = jnp.where(index == row, table_ref[row, head], weights)
    level = lax.broadcasted_iota(jnp.int32, (index.shape[0], 1), 0).astype(F32)
    return weights * jnp.exp2(-0.5 * level)


def level_pattern(size):
    s = lax.broadcasted_iota(jnp.int32, (size, size), 0)
    t = lax.broadcasted_iota(jnp.int32, (size, size), 1)
    level = jnp.zeros((size, size), jnp.int32)
    differ = s ^ t
    for bit in range(size.bit_length() - 1):
        level = level + (differ >= (1 << bit)).astype(jnp.int32)
    return jnp.where(s <= t, level, -1)


def near_tile(q, k, vt, rows, pattern):
    half = TILE // 2
    left = nt(k[:half], q)
    right = nt(k[half:], q[half:])
    mix_left = jnp.zeros((half, half), F32)
    mix_right = jnp.zeros((half, half), F32)
    for level in range(8):
        row = rows(level)
        hit = pattern == level
        mix_left = jnp.where(hit, row[:, :half], mix_left)
        mix_right = jnp.where(hit, row[:, half:], mix_right)
    top = jnp.concatenate(
        [(left[:, :half] * mix_left).astype(BF16), (left[:, half:] * rows(8)[:, half:]).astype(BF16)], axis=1
    )
    bottom = jnp.concatenate([jnp.zeros((half, half), BF16), (right * mix_right).astype(BF16)], axis=1)
    return nn(vt, jnp.concatenate([top, bottom], axis=0))


def window_tile(q, keys, vt, current, penalty):
    scores = nt(keys, q)
    previous = scores[:TILE]
    if penalty is not None:
        previous = previous + penalty
    folded = jnp.where(current, scores[TILE:], previous)
    peak = jnp.max(folded, axis=0, keepdims=True)
    exps = jnp.exp2((folded - peak) * SCORE_SCALE)
    total = jnp.sum(exps, axis=0, keepdims=True)
    exps = exps.astype(BF16)
    zero = jnp.zeros_like(exps)
    probs = jnp.concatenate([jnp.where(current, zero, exps), jnp.where(current, exps, zero)], axis=0)
    raw = nn(vt, probs)
    inverse = 1.0 / total
    mean_square = jnp.mean(raw * raw, axis=0, keepdims=True) * (inverse * inverse)
    return raw * (inverse * lax.rsqrt(mean_square + EPSILON))


def partner_of(shard, stage):
    unit = 4 ** (stage // 2)
    digit = shard // unit % 4
    other = 3 - digit if stage % 2 else digit + 1 - 2 * (digit % 2)
    return shard + (other - digit) * unit


def kernel(
    table_ref,
    lengths_ref,
    index_ref,
    gain_lin_ref,
    gain_win_ref,
    q_hbm,
    k_hbm,
    v_hbm,
    wk_hbm,
    wv_hbm,
    w_hbm,
    out_hbm,
    q_ref,
    k_ref,
    v_ref,
    vt_ref,
    wk_ref,
    wv_ref,
    wvt_ref,
    w_ref,
    weights_ref,
    tile_ref,
    run_ref,
    send_ref,
    recv_ref,
    lin_ref,
    win_ref,
    att_ref,
    part_ref,
    other_ref,
    kv_sem,
    q_sem,
    win_sem,
    w_sem,
    send_sem,
    recv_sem,
    rim_send_sem,
    rim_recv_sem,
    part_send_sem,
    part_recv_sem,
    out_sem,
):
    heads, tokens, _ = q_ref.shape
    groups = wk_ref.shape[0]
    members = heads // groups
    tiles = tokens // TILE
    stages = recv_ref.shape[1]
    own_rows = out_hbm.shape[0]
    own_tiles = own_rows // TILE
    shard_count = 1 << stages
    shard = lax.axis_index("seq")
    core = lax.axis_index("head")
    following = (shard + 1) % shard_count
    preceding = (shard + shard_count - 1) % shard_count

    def columns(hbm, h):
        return hbm.at[:, pl.ds(pl.multiple_of(h * DH, DH), DH)]

    def k_copy(h):
        return pltpu.make_async_copy(columns(k_hbm, h), k_ref.at[h], kv_sem.at[0, h])

    def v_copy(h):
        return pltpu.make_async_copy(columns(v_hbm, h), v_ref.at[h], kv_sem.at[1, h])

    def q_copy(h):
        return pltpu.make_async_copy(columns(q_hbm, h), q_ref.at[h], q_sem.at[h])

    def wk_copy(g):
        return pltpu.make_async_copy(columns(wk_hbm, g), wk_ref.at[g, pl.ds(TILE, tokens)], win_sem.at[0, g])

    def wv_copy(g):
        return pltpu.make_async_copy(columns(wv_hbm, g), wv_ref.at[g, pl.ds(TILE, tokens)], win_sem.at[1, g])

    w_copy = pltpu.make_async_copy(w_hbm, w_ref, w_sem)

    def hop(stage, h):
        return pltpu.make_async_remote_copy(
            src_ref=send_ref.at[stage, h],
            dst_ref=recv_ref.at[h, stage],
            send_sem=send_sem.at[stage, h],
            recv_sem=recv_sem.at[stage, h],
            device_id={"seq": partner_of(shard, stage)},
            device_id_type=MESH,
        )

    def rim(hbm, ref, which, g):
        return pltpu.make_async_remote_copy(
            src_ref=hbm.at[pl.ds(tokens - TILE, TILE), pl.ds(g * DH, DH)],
            dst_ref=ref.at[g, pl.ds(0, TILE)],
            send_sem=rim_send_sem.at[which, g],
            recv_sem=rim_recv_sem.at[which, g],
            device_id={"seq": following},
            device_id_type=MESH,
        )

    rims = [rim(wk_hbm, wk_ref, 0, g) for g in range(groups)] + [rim(wv_hbm, wv_ref, 1, g) for g in range(groups)]

    def part_copy(r):
        return pltpu.make_async_remote_copy(
            src_ref=part_ref.at[r],
            dst_ref=other_ref.at[r],
            send_sem=part_send_sem.at[r],
            recv_sem=part_recv_sem.at[r],
            device_id={"head": 1 - core},
            device_id_type=MESH,
        )

    def out_copy(r):
        return pltpu.make_async_copy(part_ref.at[own_tiles + r], out_hbm.at[pl.ds(r * TILE, TILE)], out_sem.at[r])

    for h in range(heads):
        k_copy(h).start()
        v_copy(h).start()
    for h in range(heads):
        q_copy(h).start()
    for g in range(groups):
        wk_copy(g).start()
        wv_copy(g).start()
    w_copy.start()

    barrier = pltpu.get_barrier_semaphore()
    for stage in range(stages):
        pl.semaphore_signal(barrier, inc=1, device_id={"seq": partner_of(shard, stage)}, device_id_type=MESH)
    pl.semaphore_signal(barrier, inc=1, device_id={"seq": preceding}, device_id_type=MESH)
    pl.semaphore_signal(barrier, inc=1, device_id={"head": 1 - core}, device_id_type=MESH)

    starts, begin, running_start = [], 0, 0
    for i in range(lengths_ref.shape[0]):
        starts.append(running_start)
        running_start = running_start + lengths_ref[i]
    for start in starts[1:]:
        begin = jnp.where(start <= shard, start, begin)
    opens_here = begin == shard

    def opened(base, span):
        found = False
        for start in starts:
            found = jnp.logical_or(found, jnp.logical_and(start >= base, start < base + span))
        return found

    keep, own_scale, partner_scale = [], [], []
    for stage in range(stages):
        span = 1 << stage
        base = shard // span * span
        upper = (shard // span) % 2 == 1
        other = jnp.where(upper, base - span, base + span)
        keep.append(jnp.where(jnp.logical_and(upper, begin < base), 1.0, 0.0))
        own_scale.append(jnp.where(jnp.logical_and(jnp.logical_not(upper), opened(other, span)), 0.0, 1.0))
        partner_scale.append(jnp.where(jnp.logical_and(upper, opened(base, span)), 0.0, 1.0))

    @pl.loop(0, heads)
    def _(h):
        weights_ref[h] = head_weights(index_ref[...], table_ref, h)

    pl.semaphore_wait(barrier, stages + 2)

    @pl.loop(0, heads)
    def _(h):
        k_copy(h).wait()
        v_copy(h).wait()
        vt_ref[h] = v_ref[h].T
        states = [
            nn(vt_ref[h, :, t * TILE : (t + 1) * TILE], k_ref[h, t * TILE : (t + 1) * TILE, :]) for t in range(tiles)
        ]
        pair = states[0] + states[1]
        tile_ref[h, 0] = states[0].astype(BF16)
        tile_ref[h, 1] = states[2].astype(BF16)
        tile_ref[h, 2] = pair.astype(BF16)
        total = pair + (states[2] + states[3])
        run_ref[h] = total
        send_ref[0, h] = total.astype(BF16)
        hop(0, h).start()

    for copy in rims:
        copy.start()

    def tick(n):
        for stage in range(stages - 1):
            h = n - LAG * stage

            @pl.when(jnp.logical_and(h >= 0, h < heads))
            def _():
                hop(stage, h).wait_recv()
                total = own_scale[stage] * run_ref[h] + partner_scale[stage] * recv_ref[h, stage].astype(F32)
                run_ref[h] = total
                send_ref[stage + 1, h] = total.astype(BF16)
                hop(stage + 1, h).start()

    for g in range(groups):
        wk_copy(g).wait()
        wv_copy(g).wait()
        wvt_ref[g, :, TILE:] = wv_ref[g, TILE:, :].T

    pattern = level_pattern(TILE // 2)
    s = lax.broadcasted_iota(jnp.int32, (TILE, TILE), 0)
    t = lax.broadcasted_iota(jnp.int32, (TILE, TILE), 1)
    current = s <= t

    def window(h, tile, penalty):
        first = tile * TILE
        g = h // members
        raw = window_tile(
            q_ref[h, first : first + TILE, :],
            wk_ref[g, first : first + 2 * TILE, :],
            wvt_ref[g, :, first : first + 2 * TILE],
            current,
            penalty,
        )
        win_ref[h, :, first : first + TILE] = raw * gain_win_ref[h].reshape(DH, 1)

    @pl.loop(0, heads)
    def _(h):
        q_copy(h).wait()
        for tile in range(tiles):
            first = tile * TILE
            q = q_ref[h, first : first + TILE, :]

            def rows(level):
                return weights_ref[h, level : level + 1, first : first + TILE]

            near = near_tile(q, k_ref[h, first : first + TILE, :], vt_ref[h, :, first : first + TILE], rows, pattern)
            if tile % 2:
                near = near + rows(9) * nt(tile_ref[h, tile // 2], q)
            if tile >= 2:
                near = near + rows(10) * nt(tile_ref[h, 2], q)
            lin_ref[h, :, first : first + TILE] = near
        tick(2 * h)
        for tile in range(1, tiles):
            window(h, tile, None)
        tick(2 * h + 1)

    for copy in rims:
        copy.wait_recv()
    for g in range(groups):
        wvt_ref[g, :, :TILE] = wv_ref[g, :TILE, :].T
    penalty = jnp.where(opens_here, -1e30, 0.0)

    @pl.loop(0, heads)
    def _(h):
        window(h, 0, penalty)

    w_copy.wait()

    @pl.loop(0, heads)
    def _(h):
        hop(stages - 1, h).wait_recv()

    @pl.loop(0, 2 * own_tiles)
    def _(r):
        mine = r // own_tiles
        first = pl.multiple_of((core + 1 - mine) % 2 * own_rows + r % own_tiles * TILE, TILE)
        span = pl.ds(first, TILE)
        for h in range(heads):
            q = q_ref[h, span, :]
            lin = lin_ref[h, :, span]
            far = nt(recv_ref[h].reshape(stages * DH, DH), q)
            for stage in range(stages):
                row = weights_ref[h, 11 + stage : 12 + stage, span] * keep[stage]
                lin = lin + row * far[stage * DH : (stage + 1) * DH]
            mean_square = jnp.mean(lin * lin, axis=0, keepdims=True)
            lin = lin * lax.rsqrt(mean_square + EPSILON) * gain_lin_ref[h].reshape(DH, 1)
            att_ref[:, h * DH : (h + 1) * DH] = (lin + win_ref[h, :, span]).astype(BF16).T
        part_ref[r] = nn(att_ref[...], w_ref[...]).astype(BF16)

        @pl.when(r < own_tiles)
        def _():
            part_copy(r).start()

        @pl.when(r >= own_tiles)
        def _():
            part_copy(r - own_tiles).wait_recv()
            part_ref[r] = (part_ref[r].astype(F32) + other_ref[r - own_tiles].astype(F32)).astype(BF16)
            out_copy(r - own_tiles).start()

    for copy in rims:
        copy.wait_send()

    @pl.loop(0, heads)
    def _(h):
        for stage in range(stages):
            hop(stage, h).wait_send()

    for r in range(own_tiles):
        part_copy(r).wait_send()
        out_copy(r).wait()


def shards(
    queries,
    lin_keys,
    lin_values,
    window_keys,
    window_values,
    level_index,
    level_table,
    seq_lengths,
    gain_linear,
    gain_window,
    w_out,
):
    tokens = queries.shape[0]
    heads = level_table.shape[1]
    groups = window_keys.shape[1] // DH
    levels = level_index.shape[0]
    tiles = tokens // TILE
    stages = lax.axis_size("seq").bit_length() - 1
    width = w_out.shape[1]
    own_rows = tokens // lax.axis_size("head")
    own_tiles = own_rows // TILE
    smem = pl.BlockSpec(memory_space=pltpu.SMEM)
    vmem = pl.BlockSpec(memory_space=pltpu.VMEM)
    hbm = pl.BlockSpec(memory_space=pl.ANY)
    dma = pltpu.SemaphoreType.DMA
    return pl.pallas_call(
        kernel,
        in_specs=[smem, smem, vmem, vmem, vmem] + [hbm] * 6,
        out_specs=hbm,
        out_shape=jax.ShapeDtypeStruct((own_rows, width), BF16),
        scratch_shapes=[
            pltpu.VMEM((heads, tokens, DH), BF16),
            pltpu.VMEM((heads, tokens, DH), BF16),
            pltpu.VMEM((heads, tokens, DH), BF16),
            pltpu.VMEM((heads, DH, tokens), BF16),
            pltpu.VMEM((groups, TILE + tokens, DH), BF16),
            pltpu.VMEM((groups, TILE + tokens, DH), BF16),
            pltpu.VMEM((groups, DH, TILE + tokens), BF16),
            pltpu.VMEM(w_out.shape, BF16),
            pltpu.VMEM((heads, levels, tokens), F32),
            pltpu.VMEM((heads, 3, DH, DH), BF16),
            pltpu.VMEM((heads, DH, DH), F32),
            pltpu.VMEM((stages, heads, DH, DH), BF16),
            pltpu.VMEM((heads, stages, DH, DH), BF16),
            pltpu.VMEM((heads, DH, tokens), F32),
            pltpu.VMEM((heads, DH, tokens), F32),
            pltpu.VMEM((TILE, heads * DH), BF16),
            pltpu.VMEM((2 * own_tiles, TILE, width), BF16),
            pltpu.VMEM((own_tiles, TILE, width), BF16),
            dma((2, heads)),
            dma((heads,)),
            dma((2, groups)),
            dma,
            dma((stages, heads)),
            dma((stages, heads)),
            dma((2, groups)),
            dma((2, groups)),
            dma((own_tiles,)),
            dma((own_tiles,)),
            dma((own_tiles,)),
        ],
        compiler_params=pltpu.CompilerParams(
            collective_id=0, has_side_effects=True, vmem_limit_bytes=60 << 20
        ),
    )(
        level_table,
        seq_lengths,
        level_index,
        gain_linear.reshape(heads, 1, DH),
        gain_window.reshape(heads, 1, DH),
        queries,
        lin_keys,
        lin_values,
        window_keys,
        window_values,
        w_out,
    )


def solution(mesh):
    placed = (
        P("seq", "head"),
        P("seq", "head"),
        P("seq", "head"),
        P("seq", "head"),
        P("seq", "head"),
        P(None, "seq"),
        P(None, "head"),
        P(),
        P("head"),
        P("head"),
        P("head", None),
    )
    return jax.shard_map(
        shards, mesh=mesh, in_specs=placed, out_specs=P(("seq", "head"), None), check_vma=False
    )
```

```python
import math

import jax
import jax.numpy as jnp
from jax import lax
from jax.experimental import pallas as pl
from jax.experimental.pallas import tpu as pltpu
from jax.sharding import PartitionSpec as P

DH = 128
TILE = 256
EPSILON = 1e-06
SCORE_SCALE = DH ** (-0.5) * math.log2(math.e)
F32 = jnp.float32
BF16 = jnp.bfloat16
MESH = pl.DeviceIdType.MESH
LAG = 6
RIM_PIECES = 4
RIM_X = 6
RIM_Y = 14


def nn(a, b):
    return jnp.dot(a, b, preferred_element_type=F32)


def head_weights(index, table_ref, head):
    weights = jnp.zeros(index.shape, F32)
    for row in range(table_ref.shape[0]):
        weights = jnp.where(index == row, table_ref[row, head], weights)
    level = lax.broadcasted_iota(jnp.int32, (index.shape[0], 1), 0).astype(F32)
    return weights * jnp.exp2(-0.5 * level)


def level_pattern(size):
    s = lax.broadcasted_iota(jnp.int32, (size, size), 0)
    t = lax.broadcasted_iota(jnp.int32, (size, size), 1)
    level = jnp.zeros((size, size), jnp.int32)
    differ = s ^ t
    for bit in range(size.bit_length() - 1):
        level = level + (differ >= (1 << bit)).astype(jnp.int32)
    return jnp.where(s <= t, level, -1)


def near_tile(qt, k, vt, rows, pattern):
    half = TILE // 2
    left = nn(k[:half], qt)
    right = nn(k[half:], qt[:, half:])
    mix_left = jnp.zeros((half, half), F32)
    mix_right = jnp.zeros((half, half), F32)
    for level in range(8):
        row = rows(level)
        hit = pattern == level
        mix_left = jnp.where(hit, row[:, :half], mix_left)
        mix_right = jnp.where(hit, row[:, half:], mix_right)
    top = jnp.concatenate(
        [(left[:, :half] * mix_left).astype(BF16), (left[:, half:] * rows(8)[:, half:]).astype(BF16)], axis=1
    )
    bottom = jnp.concatenate([jnp.zeros((half, half), BF16), (right * mix_right).astype(BF16)], axis=1)
    return nn(vt, jnp.concatenate([top, bottom], axis=0))


def window_rows(q, kt, v, current, penalty):
    n = q.shape[0]
    scores = nn(q.reshape(n * TILE, DH), kt).reshape(n, TILE, 2 * TILE)
    previous = scores[:, :, :TILE]
    if penalty is not None:
        previous = previous + penalty
    folded = jnp.where(current, scores[:, :, TILE:], previous)
    peak = jnp.max(folded, axis=2, keepdims=True)
    exps = jnp.exp2((folded - peak) * SCORE_SCALE)
    total = jnp.sum(exps, axis=2, keepdims=True)
    probs = jnp.concatenate([jnp.where(current, 0.0, exps), jnp.where(current, exps, 0.0)], axis=2).astype(BF16)
    raw = nn(probs.reshape(n * TILE, 2 * TILE), v).reshape(n, TILE, DH)
    inverse = 1.0 / total
    mean_square = jnp.mean(raw * raw, axis=2, keepdims=True) * (inverse * inverse)
    return raw * (inverse * lax.rsqrt(mean_square + EPSILON))


def partner_of(shard, stage):
    unit = 4 ** (stage // 2)
    digit = shard // unit % 4
    other = 3 - digit if stage % 2 else digit + 1 - 2 * (digit % 2)
    return shard + (other - digit) * unit


def kernel(
    table_ref,
    lengths_ref,
    index_ref,
    gain_lin_ref,
    gain_win_ref,
    q_hbm,
    k_hbm,
    v_hbm,
    wk_hbm,
    wv_hbm,
    w_hbm,
    own_hbm,
    other_hbm,
    q_ref,
    k_ref,
    v_ref,
    qt_ref,
    vt_ref,
    window_ref,
    wkt_ref,
    rim_ref,
    w_ref,
    weights_ref,
    tile_ref,
    run_ref,
    send_ref,
    recv_ref,
    lin_ref,
    win_ref,
    att_ref,
    part_ref,
    kv_sem,
    q_sem,
    win_sem,
    w_sem,
    send_sem,
    recv_sem,
    rim_load_sem,
    rim_send_sem,
    rim_recv_sem,
    part_send_sem,
    part_recv_sem,
    out_sem,
):
    heads, tokens, _ = q_ref.shape
    groups = window_ref.shape[1]
    members = heads // groups
    tiles = tokens // TILE
    stages = recv_ref.shape[1]
    own_rows = own_hbm.shape[0]
    own_tiles = own_rows // TILE
    shard = lax.axis_index("seq")
    core = lax.axis_index("head")

    def columns(hbm, h):
        return hbm.at[:, pl.ds(pl.multiple_of(h * DH, DH), DH)]

    def k_copy(h):
        return pltpu.make_async_copy(columns(k_hbm, h), k_ref.at[h], kv_sem.at[0, h])

    def v_copy(h):
        return pltpu.make_async_copy(columns(v_hbm, h), v_ref.at[h], kv_sem.at[1, h])

    def q_copy(h):
        return pltpu.make_async_copy(columns(q_hbm, h), q_ref.at[h], q_sem.at[h])

    def wk_copy(g):
        return pltpu.make_async_copy(columns(wk_hbm, g), window_ref.at[0, g, pl.ds(TILE, tokens)], win_sem.at[0, g])

    def wv_copy(g):
        return pltpu.make_async_copy(columns(wv_hbm, g), window_ref.at[1, g, pl.ds(TILE, tokens)], win_sem.at[1, g])

    w_copy = pltpu.make_async_copy(w_hbm, w_ref, w_sem)

    def hop(stage, h):
        return pltpu.make_async_remote_copy(
            src_ref=send_ref.at[stage, h],
            dst_ref=recv_ref.at[h, stage],
            send_sem=send_sem.at[stage, h],
            recv_sem=recv_sem.at[stage, h],
            device_id={"seq": partner_of(shard, stage)},
            device_id_type=MESH,
        )

    place = [shard % 4, shard // 4 % 4, shard // 16]
    rim_count = groups * RIM_PIECES
    last_y = place[0] == 3
    on_leg = [last_y, jnp.logical_and(last_y, place[1] == 0), place[0] >= 0]
    from_z = jnp.logical_and(last_y, place[1] > 0)
    rim_slot = jnp.where(on_leg[1], 2, jnp.where(last_y, 1, 0))

    def rim(leg, n):
        rows = TILE // RIM_PIECES
        g, piece = n // RIM_PIECES, n % RIM_PIECES
        span = pl.ds(pl.multiple_of(piece * rows, rows), rows)
        axis = (1, 2, 0)[leg]
        return pltpu.make_async_remote_copy(
            src_ref=rim_ref.at[(0, 1, rim_slot)[leg], :, g, span],
            dst_ref=rim_ref.at[leg + 1, :, g, span],
            send_sem=rim_send_sem.at[leg, n],
            recv_sem=rim_recv_sem.at[leg, n],
            device_id={"seq": shard + ((place[axis] + 1) % 4 - place[axis]) * 4**axis},
            device_id_type=MESH,
        )

    def rim_load(which, g):
        hbm = (wk_hbm, wv_hbm)[which]
        return pltpu.make_async_copy(
            hbm.at[pl.ds(tokens - TILE, TILE), pl.ds(g * DH, DH)], rim_ref.at[0, which, g], rim_load_sem.at[which, g]
        )

    def part_copy(r):
        return pltpu.make_async_remote_copy(
            src_ref=part_ref.at[r],
            dst_ref=other_hbm.at[pl.ds(r * TILE, TILE)],
            send_sem=part_send_sem.at[r],
            recv_sem=part_recv_sem.at[r],
            device_id={"head": 1 - core},
            device_id_type=MESH,
        )

    def out_copy(r):
        return pltpu.make_async_copy(part_ref.at[own_tiles + r], own_hbm.at[pl.ds(r * TILE, TILE)], out_sem.at[r])

    for h in range(heads):
        k_copy(h).start()
        v_copy(h).start()
    for g in range(groups):
        for which in range(2):
            rim_load(which, g).start()
    for h in range(heads):
        q_copy(h).start()
    for g in range(groups):
        wk_copy(g).start()
        wv_copy(g).start()
    w_copy.start()

    barrier = pltpu.get_barrier_semaphore()
    for stage in range(stages):
        pl.semaphore_signal(barrier, inc=1, device_id={"seq": partner_of(shard, stage)}, device_id_type=MESH)
    pl.semaphore_signal(barrier, inc=1, device_id={"head": 1 - core}, device_id_type=MESH)

    starts, begin, running_start = [], 0, 0
    for i in range(lengths_ref.shape[0]):
        starts.append(running_start)
        running_start = running_start + lengths_ref[i]
    for start in starts[1:]:
        begin = jnp.where(start <= shard, start, begin)
    opens_here = begin == shard

    def opened(base, span):
        found = False
        for start in starts:
            found = jnp.logical_or(found, jnp.logical_and(start >= base, start < base + span))
        return found

    keep, own_scale, partner_scale = [], [], []
    for stage in range(stages):
        span = 1 << stage
        base = shard // span * span
        upper = (shard // span) % 2 == 1
        other = jnp.where(upper, base - span, base + span)
        keep.append(jnp.where(jnp.logical_and(upper, begin < base), 1.0, 0.0))
        own_scale.append(jnp.where(jnp.logical_and(jnp.logical_not(upper), opened(other, span)), 0.0, 1.0))
        partner_scale.append(jnp.where(jnp.logical_and(upper, opened(base, span)), 0.0, 1.0))

    @pl.loop(0, heads)
    def _(h):
        weights_ref[h] = head_weights(index_ref[...], table_ref, h)

    for g in range(groups):
        for which in range(2):
            rim_load(which, g).wait()
    pl.semaphore_wait(barrier, stages + 1)

    @pl.when(on_leg[0])
    def _():
        @pl.loop(0, rim_count)
        def _(n):
            rim(0, n).start()


    @pl.loop(0, heads)
    def _(h):
        k_copy(h).wait()
        v_copy(h).wait()
        vt_ref[h] = v_ref[h].T
        states = [
            nn(vt_ref[h, :, t * TILE : (t + 1) * TILE], k_ref[h, t * TILE : (t + 1) * TILE, :]) for t in range(tiles)
        ]
        pair = states[0] + states[1]
        tile_ref[h, 0] = states[0].astype(BF16)
        tile_ref[h, 1] = states[2].astype(BF16)
        tile_ref[h, 2] = pair.astype(BF16)
        total = pair + (states[2] + states[3])
        run_ref[h] = total
        send_ref[0, h] = total.astype(BF16)
        hop(0, h).start()

    def tick(n):
        for stage in range(stages - 1):
            h = n - LAG * stage

            @pl.when(jnp.logical_and(h >= 0, h < heads))
            def _():
                hop(stage, h).wait_recv()
                total = own_scale[stage] * run_ref[h] + partner_scale[stage] * recv_ref[h, stage].astype(F32)
                run_ref[h] = total
                send_ref[stage + 1, h] = total.astype(BF16)
                hop(stage + 1, h).start()

        piece = n - RIM_X

        @pl.when(jnp.logical_and(on_leg[1], jnp.logical_and(piece >= 0, piece < rim_count)))
        def _():
            rim(0, piece).wait_recv()
            rim(1, piece).start()

        last = n - RIM_Y

        @pl.when(jnp.logical_and(last >= 0, last < rim_count))
        def _():
            @pl.when(from_z)
            def _():
                rim(0, last).wait_recv()

            @pl.when(on_leg[1])
            def _():
                rim(1, last).wait_recv()

            rim(2, last).start()

    for g in range(groups):
        wk_copy(g).wait()
        wv_copy(g).wait()
        for tile in range(1, tiles + 1):
            wkt_ref[g, tile] = window_ref[0, g, tile * TILE : (tile + 1) * TILE, :].T

    pattern = level_pattern(TILE // 2)
    t = lax.broadcasted_iota(jnp.int32, (TILE, TILE), 0)
    s = lax.broadcasted_iota(jnp.int32, (TILE, TILE), 1)
    current = s <= t

    def near(h, tile):
        first = tile * TILE
        qt = qt_ref[h, :, first : first + TILE]

        def rows(level):
            return weights_ref[h, level : level + 1, first : first + TILE]

        total = near_tile(qt, k_ref[h, first : first + TILE, :], vt_ref[h, :, first : first + TILE], rows, pattern)
        if tile % 2:
            total = total + rows(9) * nn(tile_ref[h, tile // 2], qt)
        if tile >= 2:
            total = total + rows(10) * nn(tile_ref[h, 2], qt)
        lin_ref[h, :, first : first + TILE] = total

    def window(g, tile, penalty):
        first = tile * TILE if isinstance(tile, int) else pl.multiple_of(tile * TILE, TILE)
        mine = pl.ds(g * members, members)
        raw = window_rows(
            q_ref[mine, pl.ds(first, TILE), :],
            jnp.concatenate([wkt_ref[g, tile], wkt_ref[g, tile + 1]], axis=1),
            window_ref[1, g, pl.ds(first, 2 * TILE), :],
            current,
            penalty,
        )
        win_ref[mine, pl.ds(first, TILE), :] = raw * gain_win_ref[mine]

    def far(h, tile, first_stage, last_stage):
        first = tile * TILE
        qt = qt_ref[h, :, first : first + TILE]
        count = last_stage - first_stage
        reached = nn(recv_ref[h, first_stage:last_stage].reshape(count * DH, DH), qt)
        lin = lin_ref[h, :, first : first + TILE]
        for i in range(count):
            level = 11 + first_stage + i
            row = weights_ref[h, level : level + 1, first : first + TILE] * keep[first_stage + i]
            lin = lin + row * reached[i * DH : (i + 1) * DH]
        return lin

    for h in range(heads):
        q_copy(h).wait()

    @pl.loop(0, heads)
    def _(i):
        qt_ref[i] = q_ref[i].T
        near(i, 0)
        near(i, 1)
        tick(3 * i)

        near(i, 2)
        near(i, 3)
        tick(3 * i + 1)

        @pl.when(i < groups * (tiles - 1))
        def _():
            window(i % groups, 1 + i // groups, None)

        tick(3 * i + 2)

    early = stages - 2

    @pl.loop(0, heads)
    def _(h):
        for tile in range(tiles):
            lin_ref[h, :, tile * TILE : (tile + 1) * TILE] = far(h, tile, 0, early)
        tick(3 * heads + h)

    @pl.loop(0, rim_count)
    def _(n):
        rim(2, n).wait_recv()

    for g in range(groups):
        wkt_ref[g, 0] = rim_ref[3, 0, g].T
        window_ref[1, g, :TILE, :] = rim_ref[3, 1, g]
        window(g, 0, jnp.where(opens_here, -1e30, 0.0))

    @pl.loop(0, heads)
    def _(h):
        hop(stages - 1, h).wait_recv()
        for tile in range(tiles):
            span = pl.ds(tile * TILE, TILE)
            lin = far(h, tile, early, stages)
            mean_square = jnp.mean(lin * lin, axis=0, keepdims=True)
            lin = (lin * lax.rsqrt(mean_square + EPSILON)).T * gain_lin_ref[h]
            att_ref[span, pl.ds(pl.multiple_of(h * DH, DH), DH)] = (lin + win_ref[h, span, :]).astype(BF16)

    w_copy.wait()

    @pl.loop(0, 2 * own_tiles)
    def _(r):
        mine = r // own_tiles
        first = pl.multiple_of((core + 1 - mine) % 2 * own_rows + r % own_tiles * TILE, TILE)
        part_ref[r] = nn(att_ref[pl.ds(first, TILE), :], w_ref[...]).astype(BF16)

        @pl.when(r < own_tiles)
        def _():
            part_copy(r).start()

        @pl.when(r >= own_tiles)
        def _():
            out_copy(r - own_tiles).start()

    for leg in range(3):

        @pl.when(on_leg[leg])
        def _():
            @pl.loop(0, rim_count)
            def _(n):
                rim(leg, n).wait_send()

    @pl.loop(0, heads)
    def _(h):
        for stage in range(stages):
            hop(stage, h).wait_send()

    for r in range(own_tiles):
        part_copy(r).wait()
        out_copy(r).wait()


def shards(
    queries,
    lin_keys,
    lin_values,
    window_keys,
    window_values,
    level_index,
    level_table,
    seq_lengths,
    gain_linear,
    gain_window,
    w_out,
):
    tokens = queries.shape[0]
    heads = level_table.shape[1]
    groups = window_keys.shape[1] // DH
    levels = level_index.shape[0]
    tiles = tokens // TILE
    stages = lax.axis_size("seq").bit_length() - 1
    width = w_out.shape[1]
    own_rows = tokens // lax.axis_size("head")
    own_tiles = own_rows // TILE
    smem = pl.BlockSpec(memory_space=pltpu.SMEM)
    vmem = pl.BlockSpec(memory_space=pltpu.VMEM)
    hbm = pl.BlockSpec(memory_space=pl.ANY)
    dma = pltpu.SemaphoreType.DMA
    own, other = pl.pallas_call(
        kernel,
        in_specs=[smem, smem, vmem, vmem, vmem] + [hbm] * 6,
        out_specs=[hbm] * 2,
        out_shape=[jax.ShapeDtypeStruct((own_rows, width), BF16)] * 2,
        scratch_shapes=[
            pltpu.VMEM((heads, tokens, DH), BF16),
            pltpu.VMEM((heads, tokens, DH), BF16),
            pltpu.VMEM((heads, tokens, DH), BF16),
            pltpu.VMEM((heads, DH, tokens), BF16),
            pltpu.VMEM((heads, DH, tokens), BF16),
            pltpu.VMEM((2, groups, TILE + tokens, DH), BF16),
            pltpu.VMEM((groups, tiles + 1, DH, TILE), BF16),
            pltpu.VMEM((4, 2, groups, TILE, DH), BF16),
            pltpu.VMEM(w_out.shape, BF16),
            pltpu.VMEM((heads, levels, tokens), F32),
            pltpu.VMEM((heads, 3, DH, DH), BF16),
            pltpu.VMEM((heads, DH, DH), F32),
            pltpu.VMEM((stages, heads, DH, DH), BF16),
            pltpu.VMEM((heads, stages, DH, DH), BF16),
            pltpu.VMEM((heads, DH, tokens), F32),
            pltpu.VMEM((heads, tokens, DH), F32),
            pltpu.VMEM((tokens, heads * DH), BF16),
            pltpu.VMEM((2 * own_tiles, TILE, width), BF16),
            dma((2, heads)),
            dma((heads,)),
            dma((2, groups)),
            dma,
            dma((stages, heads)),
            dma((stages, heads)),
            dma((2, groups)),
            dma((3, groups * RIM_PIECES)),
            dma((3, groups * RIM_PIECES)),
            dma((own_tiles,)),
            dma((own_tiles,)),
            dma((own_tiles,)),
        ],
        compiler_params=pltpu.CompilerParams(
            collective_id=0, has_side_effects=True, vmem_limit_bytes=60 << 20
        ),
    )(
        level_table,
        seq_lengths,
        level_index,
        gain_linear.reshape(heads, 1, DH),
        gain_window.reshape(heads, 1, DH),
        queries,
        lin_keys,
        lin_values,
        window_keys,
        window_values,
        w_out,
    )
    return (own.astype(F32) + other.astype(F32)).astype(BF16)


def solution(mesh):
    placed = (
        P("seq", "head"),
        P("seq", "head"),
        P("seq", "head"),
        P("seq", "head"),
        P("seq", "head"),
        P(None, "seq"),
        P(None, "head"),
        P(),
        P("head"),
        P("head"),
        P("head", None),
    )
    return jax.shard_map(
        shards, mesh=mesh, in_specs=placed, out_specs=P(("seq", "head"), None), check_vma=False
    )
```

```python
import math

import jax
import jax.numpy as jnp
from jax import lax
from jax.experimental import pallas as pl
from jax.experimental.pallas import tpu as pltpu
from jax.sharding import PartitionSpec as P

DH = 128
TILE = 256
EPSILON = 1e-06
SCORE_SCALE = DH ** (-0.5) * math.log2(math.e)
F32 = jnp.float32
BF16 = jnp.bfloat16
MESH = pl.DeviceIdType.MESH
LAG = 6
RIM_PIECES = 4
RIM_X = 6
RIM_Y = 14


def nn(a, b):
    return jnp.dot(a, b, preferred_element_type=F32)


def head_weights(index, table_ref, head):
    weights = jnp.zeros(index.shape, F32)
    for row in range(table_ref.shape[0]):
        weights = jnp.where(index == row, table_ref[row, head], weights)
    level = lax.broadcasted_iota(jnp.int32, (index.shape[0], 1), 0).astype(F32)
    return weights * jnp.exp2(-0.5 * level)


def level_pattern(size):
    s = lax.broadcasted_iota(jnp.int32, (size, size), 0)
    t = lax.broadcasted_iota(jnp.int32, (size, size), 1)
    level = jnp.zeros((size, size), jnp.int32)
    differ = s ^ t
    for bit in range(size.bit_length() - 1):
        level = level + (differ >= (1 << bit)).astype(jnp.int32)
    return jnp.where(s <= t, level, -1)


def near_tile(qt, k, vt, rows, pattern):
    half = TILE // 2
    left = nn(k[:half], qt)
    right = nn(k[half:], qt[:, half:])
    mix_left = jnp.zeros((half, half), F32)
    mix_right = jnp.zeros((half, half), F32)
    for level in range(8):
        row = rows(level)
        hit = pattern == level
        mix_left = jnp.where(hit, row[:, :half], mix_left)
        mix_right = jnp.where(hit, row[:, half:], mix_right)
    top = jnp.concatenate(
        [(left[:, :half] * mix_left).astype(BF16), (left[:, half:] * rows(8)[:, half:]).astype(BF16)], axis=1
    )
    bottom = jnp.concatenate([jnp.zeros((half, half), BF16), (right * mix_right).astype(BF16)], axis=1)
    return nn(vt, jnp.concatenate([top, bottom], axis=0))


def window_rows(q, kt, v, current, penalty):
    n = q.shape[0]
    scores = nn(q.reshape(n * TILE, DH), kt).reshape(n, TILE, 2 * TILE)
    previous = scores[:, :, :TILE]
    if penalty is not None:
        previous = previous + penalty
    folded = jnp.where(current, scores[:, :, TILE:], previous)
    peak = jnp.max(folded, axis=2, keepdims=True)
    exps = jnp.exp2((folded - peak) * SCORE_SCALE)
    total = jnp.sum(exps, axis=2, keepdims=True)
    probs = jnp.concatenate([jnp.where(current, 0.0, exps), jnp.where(current, exps, 0.0)], axis=2).astype(BF16)
    raw = nn(probs.reshape(n * TILE, 2 * TILE), v).reshape(n, TILE, DH)
    inverse = 1.0 / total
    mean_square = jnp.mean(raw * raw, axis=2, keepdims=True) * (inverse * inverse)
    return raw * (inverse * lax.rsqrt(mean_square + EPSILON))


def partner_of(shard, stage):
    unit = 4 ** (stage // 2)
    digit = shard // unit % 4
    other = 3 - digit if stage % 2 else digit + 1 - 2 * (digit % 2)
    return shard + (other - digit) * unit


def kernel(
    table_hbm,
    lengths_hbm,
    index_hbm,
    gain_lin_hbm,
    gain_win_hbm,
    q_hbm,
    k_hbm,
    v_hbm,
    wk_hbm,
    wv_hbm,
    w_hbm,
    own_ref,
    other_ref,
    table_ref,
    lengths_ref,
    index_ref,
    gain_lin_ref,
    gain_win_ref,
    q_ref,
    k_ref,
    v_ref,
    qt_ref,
    vt_ref,
    window_ref,
    wkt_ref,
    rim_ref,
    w_ref,
    weights_ref,
    tile_ref,
    run_ref,
    send_ref,
    recv_ref,
    lin_ref,
    win_ref,
    att_ref,
    part_ref,
    small_sem,
    kv_sem,
    q_sem,
    win_sem,
    w_sem,
    send_sem,
    recv_sem,
    rim_load_sem,
    rim_send_sem,
    rim_recv_sem,
    part_send_sem,
    part_recv_sem,
):
    heads, tokens, _ = q_ref.shape
    groups = window_ref.shape[1]
    members = heads // groups
    tiles = tokens // TILE
    stages = recv_ref.shape[1]
    own_rows = own_ref.shape[0]
    own_tiles = own_rows // TILE
    shard = lax.axis_index("seq")
    core = lax.axis_index("head")

    def columns(hbm, h):
        return hbm.at[:, pl.ds(pl.multiple_of(h * DH, DH), DH)]

    def k_copy(h):
        return pltpu.make_async_copy(columns(k_hbm, h), k_ref.at[h], kv_sem.at[0, h])

    def v_copy(h):
        return pltpu.make_async_copy(columns(v_hbm, h), v_ref.at[h], kv_sem.at[1, h])

    def q_copy(h):
        return pltpu.make_async_copy(columns(q_hbm, h), q_ref.at[h], q_sem.at[h])

    def wk_copy(g):
        return pltpu.make_async_copy(columns(wk_hbm, g), window_ref.at[0, g, pl.ds(TILE, tokens)], win_sem.at[0, g])

    def wv_copy(g):
        return pltpu.make_async_copy(columns(wv_hbm, g), window_ref.at[1, g, pl.ds(TILE, tokens)], win_sem.at[1, g])

    w_copy = pltpu.make_async_copy(w_hbm, w_ref, w_sem)

    def hop(stage, h):
        return pltpu.make_async_remote_copy(
            src_ref=send_ref.at[stage, h],
            dst_ref=recv_ref.at[h, stage],
            send_sem=send_sem.at[stage, h],
            recv_sem=recv_sem.at[stage, h],
            device_id={"seq": partner_of(shard, stage)},
            device_id_type=MESH,
        )

    place = [shard % 4, shard // 4 % 4, shard // 16]
    rim_count = groups * RIM_PIECES
    last_y = place[0] == 3
    on_leg = [last_y, jnp.logical_and(last_y, place[1] == 0), place[0] >= 0]
    from_z = jnp.logical_and(last_y, place[1] > 0)
    rim_slot = jnp.where(on_leg[1], 2, jnp.where(last_y, 1, 0))

    def rim(leg, n):
        rows = TILE // RIM_PIECES
        g, piece = n // RIM_PIECES, n % RIM_PIECES
        span = pl.ds(pl.multiple_of(piece * rows, rows), rows)
        axis = (1, 2, 0)[leg]
        return pltpu.make_async_remote_copy(
            src_ref=rim_ref.at[(0, 1, rim_slot)[leg], :, g, span],
            dst_ref=rim_ref.at[leg + 1, :, g, span],
            send_sem=rim_send_sem.at[leg, n],
            recv_sem=rim_recv_sem.at[leg, n],
            device_id={"seq": shard + ((place[axis] + 1) % 4 - place[axis]) * 4**axis},
            device_id_type=MESH,
        )

    def rim_load(which, g):
        hbm = (wk_hbm, wv_hbm)[which]
        return pltpu.make_async_copy(
            hbm.at[pl.ds(tokens - TILE, TILE), pl.ds(g * DH, DH)], rim_ref.at[0, which, g], rim_load_sem.at[which, g]
        )

    def part_copy(r):
        return pltpu.make_async_remote_copy(
            src_ref=part_ref.at[r],
            dst_ref=other_ref.at[pl.ds(r * TILE, TILE)],
            send_sem=part_send_sem.at[r],
            recv_sem=part_recv_sem.at[r],
            device_id={"head": 1 - core},
            device_id_type=MESH,
        )

    small = [
        pltpu.make_async_copy(hbm, ref, small_sem.at[n])
        for n, (hbm, ref) in enumerate(
            (
                (lengths_hbm, lengths_ref),
                (table_hbm, table_ref),
                (index_hbm, index_ref),
                (gain_lin_hbm, gain_lin_ref),
                (gain_win_hbm, gain_win_ref),
            )
        )
    ]
    for h in range(heads):
        k_copy(h).start()
        v_copy(h).start()
    for copy in small:
        copy.start()
    for g in range(groups):
        for which in range(2):
            rim_load(which, g).start()
    for h in range(heads):
        q_copy(h).start()
    for g in range(groups):
        wk_copy(g).start()
        wv_copy(g).start()
    w_copy.start()

    barrier = pltpu.get_barrier_semaphore()
    for stage in range(stages):
        pl.semaphore_signal(barrier, inc=1, device_id={"seq": partner_of(shard, stage)}, device_id_type=MESH)
    pl.semaphore_signal(barrier, inc=1, device_id={"head": 1 - core}, device_id_type=MESH)

    def state(h):
        k_copy(h).wait()
        v_copy(h).wait()
        vt_ref[h] = v_ref[h].T
        states = [
            nn(vt_ref[h, :, t * TILE : (t + 1) * TILE], k_ref[h, t * TILE : (t + 1) * TILE, :]) for t in range(tiles)
        ]
        pair = states[0] + states[1]
        tile_ref[h, 0] = states[0].astype(BF16)
        tile_ref[h, 1] = states[2].astype(BF16)
        tile_ref[h, 2] = pair.astype(BF16)
        total = pair + (states[2] + states[3])
        run_ref[h] = total
        send_ref[0, h] = total.astype(BF16)

    state(0)
    pl.semaphore_wait(barrier, stages + 1)
    hop(0, 0).start()

    @pl.loop(1, heads)
    def _(h):
        state(h)
        hop(0, h).start()

    for g in range(groups):
        for which in range(2):
            rim_load(which, g).wait()

    @pl.when(on_leg[0])
    def _():
        @pl.loop(0, rim_count)
        def _(n):
            rim(0, n).start()

    for copy in small:
        copy.wait()

    starts, begin, running_start = [], 0, 0
    for i in range(lengths_ref.shape[0]):
        starts.append(running_start)
        running_start = running_start + lengths_ref[i]
    for start in starts[1:]:
        begin = jnp.where(start <= shard, start, begin)
    opens_here = begin == shard

    def opened(base, span):
        found = False
        for start in starts:
            found = jnp.logical_or(found, jnp.logical_and(start >= base, start < base + span))
        return found

    keep, own_scale, partner_scale = [], [], []
    for stage in range(stages):
        span = 1 << stage
        base = shard // span * span
        upper = (shard // span) % 2 == 1
        other = jnp.where(upper, base - span, base + span)
        keep.append(jnp.where(jnp.logical_and(upper, begin < base), 1.0, 0.0))
        own_scale.append(jnp.where(jnp.logical_and(jnp.logical_not(upper), opened(other, span)), 0.0, 1.0))
        partner_scale.append(jnp.where(jnp.logical_and(upper, opened(base, span)), 0.0, 1.0))

    @pl.loop(0, heads)
    def _(h):
        weights_ref[h] = head_weights(index_ref[...], table_ref, h)

    def tick(n):
        for stage in range(stages - 1):
            h = n - LAG * stage

            @pl.when(jnp.logical_and(h >= 0, h < heads))
            def _():
                hop(stage, h).wait_recv()
                total = own_scale[stage] * run_ref[h] + partner_scale[stage] * recv_ref[h, stage].astype(F32)
                run_ref[h] = total
                send_ref[stage + 1, h] = total.astype(BF16)
                hop(stage + 1, h).start()

        piece = n - RIM_X

        @pl.when(jnp.logical_and(on_leg[1], jnp.logical_and(piece >= 0, piece < rim_count)))
        def _():
            rim(0, piece).wait_recv()
            rim(1, piece).start()

        last = n - RIM_Y

        @pl.when(jnp.logical_and(last >= 0, last < rim_count))
        def _():
            @pl.when(from_z)
            def _():
                rim(0, last).wait_recv()

            @pl.when(on_leg[1])
            def _():
                rim(1, last).wait_recv()

            rim(2, last).start()

    for g in range(groups):
        wk_copy(g).wait()
        wv_copy(g).wait()
        for tile in range(1, tiles + 1):
            wkt_ref[g, tile] = window_ref[0, g, tile * TILE : (tile + 1) * TILE, :].T

    pattern = level_pattern(TILE // 2)
    t = lax.broadcasted_iota(jnp.int32, (TILE, TILE), 0)
    s = lax.broadcasted_iota(jnp.int32, (TILE, TILE), 1)
    current = s <= t

    def near(h, tile):
        first = tile * TILE
        qt = qt_ref[h, :, first : first + TILE]

        def rows(level):
            return weights_ref[h, level : level + 1, first : first + TILE]

        total = near_tile(qt, k_ref[h, first : first + TILE, :], vt_ref[h, :, first : first + TILE], rows, pattern)
        if tile % 2:
            total = total + rows(9) * nn(tile_ref[h, tile // 2], qt)
        if tile >= 2:
            total = total + rows(10) * nn(tile_ref[h, 2], qt)
        lin_ref[h, :, first : first + TILE] = total

    def window(g, tile, penalty):
        first = tile * TILE if isinstance(tile, int) else pl.multiple_of(tile * TILE, TILE)
        mine = pl.ds(g * members, members)
        raw = window_rows(
            q_ref[mine, pl.ds(first, TILE), :],
            jnp.concatenate([wkt_ref[g, tile], wkt_ref[g, tile + 1]], axis=1),
            window_ref[1, g, pl.ds(first, 2 * TILE), :],
            current,
            penalty,
        )
        win_ref[mine, pl.ds(first, TILE), :] = raw * gain_win_ref[mine]

    def far(h, tile, first_stage, last_stage):
        first = tile * TILE
        qt = qt_ref[h, :, first : first + TILE]
        count = last_stage - first_stage
        reached = nn(recv_ref[h, first_stage:last_stage].reshape(count * DH, DH), qt)
        lin = lin_ref[h, :, first : first + TILE]
        for i in range(count):
            level = 11 + first_stage + i
            row = weights_ref[h, level : level + 1, first : first + TILE] * keep[first_stage + i]
            lin = lin + row * reached[i * DH : (i + 1) * DH]
        return lin

    for h in range(heads):
        q_copy(h).wait()

    @pl.loop(0, heads)
    def _(i):
        qt_ref[i] = q_ref[i].T
        near(i, 0)
        near(i, 1)
        tick(3 * i)

        near(i, 2)
        near(i, 3)
        tick(3 * i + 1)

        @pl.when(i < groups * (tiles - 1))
        def _():
            window(i % groups, 1 + i // groups, None)

        tick(3 * i + 2)

    early = stages - 2

    @pl.loop(0, heads)
    def _(h):
        for tile in range(tiles):
            lin_ref[h, :, tile * TILE : (tile + 1) * TILE] = far(h, tile, 0, early)
        tick(3 * heads + h)

    @pl.loop(0, rim_count)
    def _(n):
        rim(2, n).wait_recv()

    for g in range(groups):
        wkt_ref[g, 0] = rim_ref[3, 0, g].T
        window_ref[1, g, :TILE, :] = rim_ref[3, 1, g]
        window(g, 0, jnp.where(opens_here, -1e30, 0.0))

    @pl.loop(0, heads)
    def _(h):
        hop(stages - 1, h).wait_recv()
        for tile in range(tiles):
            span = pl.ds(tile * TILE, TILE)
            lin = far(h, tile, early, stages)
            mean_square = jnp.mean(lin * lin, axis=0, keepdims=True)
            lin = (lin * lax.rsqrt(mean_square + EPSILON)).T * gain_lin_ref[h]
            att_ref[span, pl.ds(pl.multiple_of(h * DH, DH), DH)] = (lin + win_ref[h, span, :]).astype(BF16)

    w_copy.wait()

    def project(owner, r):
        first = pl.multiple_of(owner * own_rows + r * TILE, TILE)
        return nn(att_ref[pl.ds(first, TILE), :], w_ref[...]).astype(BF16)

    @pl.loop(0, own_tiles)
    def _(r):
        part_ref[r] = project(1 - core, r)
        part_copy(r).start()

    @pl.loop(0, own_tiles)
    def _(r):
        own_ref[pl.ds(pl.multiple_of(r * TILE, TILE), TILE), :] = project(core, r)

    for leg in range(3):

        @pl.when(on_leg[leg])
        def _():
            @pl.loop(0, rim_count)
            def _(n):
                rim(leg, n).wait_send()

    @pl.loop(0, heads)
    def _(h):
        for stage in range(stages):
            hop(stage, h).wait_send()

    for r in range(own_tiles):
        part_copy(r).wait()


def shards(
    queries,
    lin_keys,
    lin_values,
    window_keys,
    window_values,
    level_index,
    level_table,
    seq_lengths,
    gain_linear,
    gain_window,
    w_out,
):
    tokens = queries.shape[0]
    heads = level_table.shape[1]
    groups = window_keys.shape[1] // DH
    levels = level_index.shape[0]
    tiles = tokens // TILE
    stages = lax.axis_size("seq").bit_length() - 1
    width = w_out.shape[1]
    own_rows = tokens // lax.axis_size("head")
    own_tiles = own_rows // TILE
    vmem = pl.BlockSpec(memory_space=pltpu.VMEM)
    hbm = pl.BlockSpec(memory_space=pltpu.HBM)
    dma = pltpu.SemaphoreType.DMA
    own, other = pl.pallas_call(
        kernel,
        in_specs=[hbm] * 11,
        out_specs=[vmem] * 2,
        out_shape=[pltpu.VMEM((own_rows, width), BF16)] * 2,
        scratch_shapes=[
            pltpu.SMEM(level_table.shape, F32),
            pltpu.SMEM(seq_lengths.shape, jnp.int32),
            pltpu.VMEM(level_index.shape, jnp.int32),
            pltpu.VMEM((heads, 1, DH), F32),
            pltpu.VMEM((heads, 1, DH), F32),
            pltpu.VMEM((heads, tokens, DH), BF16),
            pltpu.VMEM((heads, tokens, DH), BF16),
            pltpu.VMEM((heads, tokens, DH), BF16),
            pltpu.VMEM((heads, DH, tokens), BF16),
            pltpu.VMEM((heads, DH, tokens), BF16),
            pltpu.VMEM((2, groups, TILE + tokens, DH), BF16),
            pltpu.VMEM((groups, tiles + 1, DH, TILE), BF16),
            pltpu.VMEM((4, 2, groups, TILE, DH), BF16),
            pltpu.VMEM(w_out.shape, BF16),
            pltpu.VMEM((heads, levels, tokens), F32),
            pltpu.VMEM((heads, 3, DH, DH), BF16),
            pltpu.VMEM((heads, DH, DH), F32),
            pltpu.VMEM((stages, heads, DH, DH), BF16),
            pltpu.VMEM((heads, stages, DH, DH), BF16),
            pltpu.VMEM((heads, DH, tokens), F32),
            pltpu.VMEM((heads, tokens, DH), F32),
            pltpu.VMEM((tokens, heads * DH), BF16),
            pltpu.VMEM((own_tiles, TILE, width), BF16),
            dma((5,)),
            dma((2, heads)),
            dma((heads,)),
            dma((2, groups)),
            dma,
            dma((stages, heads)),
            dma((stages, heads)),
            dma((2, groups)),
            dma((3, groups * RIM_PIECES)),
            dma((3, groups * RIM_PIECES)),
            dma((own_tiles,)),
            dma((own_tiles,)),
        ],
        compiler_params=pltpu.CompilerParams(
            collective_id=0, has_side_effects=True, vmem_limit_bytes=48 << 20
        ),
    )(
        *(
            pltpu.with_memory_space_constraint(x, pltpu.HBM)
            for x in (
                level_table,
                seq_lengths,
                level_index,
                gain_linear.reshape(heads, 1, DH),
                gain_window.reshape(heads, 1, DH),
                queries,
                lin_keys,
                lin_values,
                window_keys,
                window_values,
                w_out,
            )
        )
    )
    return (own.astype(F32) + other.astype(F32)).astype(BF16)


def solution(mesh):
    placed = (
        P("seq", "head"),
        P("seq", "head"),
        P("seq", "head"),
        P("seq", "head"),
        P("seq", "head"),
        P(None, "seq"),
        P(None, "head"),
        P(),
        P("head"),
        P("head"),
        P("head", None),
    )
    return jax.shard_map(
        shards, mesh=mesh, in_specs=placed, out_specs=P(("seq", "head"), None), check_vma=False
    )
```

```python
import math

import jax
import jax.numpy as jnp
from jax import lax
from jax.experimental import pallas as pl
from jax.experimental.pallas import tpu as pltpu
from jax.sharding import PartitionSpec as P

DH = 128
TILE = 256
EPSILON = 1e-06
SCORE_SCALE = DH ** (-0.5) * math.log2(math.e)
F32 = jnp.float32
BF16 = jnp.bfloat16
MESH = pl.DeviceIdType.MESH
LAG = 6
RIM_PIECES = 2
RIM_X = 6
RIM_Y = 14


def nn(a, b):
    return jnp.dot(a, b, preferred_element_type=F32)


def head_weights(index, table_ref, head):
    weights = jnp.zeros(index.shape, F32)
    for row in range(table_ref.shape[0]):
        weights = jnp.where(index == row, table_ref[row, head], weights)
    level = lax.broadcasted_iota(jnp.int32, (index.shape[0], 1), 0).astype(F32)
    return weights * jnp.exp2(-0.5 * level)


def level_pattern(size):
    s = lax.broadcasted_iota(jnp.int32, (size, size), 0)
    t = lax.broadcasted_iota(jnp.int32, (size, size), 1)
    level = jnp.zeros((size, size), jnp.int32)
    differ = s ^ t
    for bit in range(size.bit_length() - 1):
        level = level + (differ >= (1 << bit)).astype(jnp.int32)
    return jnp.where(s <= t, level, -1)


def near_tile(qt, k, vt, rows, pattern):
    half = TILE // 2
    left = nn(k[:half], qt)
    right = nn(k[half:], qt[:, half:])
    mix_left = jnp.zeros((half, half), F32)
    mix_right = jnp.zeros((half, half), F32)
    for level in range(8):
        row = rows(level)
        hit = pattern == level
        mix_left = jnp.where(hit, row[:, :half], mix_left)
        mix_right = jnp.where(hit, row[:, half:], mix_right)
    top = jnp.concatenate(
        [(left[:, :half] * mix_left).astype(BF16), (left[:, half:] * rows(8)[:, half:]).astype(BF16)], axis=1
    )
    bottom = jnp.concatenate([jnp.zeros((half, half), BF16), (right * mix_right).astype(BF16)], axis=1)
    return nn(vt, jnp.concatenate([top, bottom], axis=0))


def window_rows(q, kt, v, current, penalty):
    n = q.shape[0]
    scores = nn(q.reshape(n * TILE, DH), kt).reshape(n, TILE, 2 * TILE)
    previous = scores[:, :, :TILE]
    if penalty is not None:
        previous = previous + penalty
    folded = jnp.where(current, scores[:, :, TILE:], previous)
    peak = jnp.max(folded, axis=2, keepdims=True)
    exps = jnp.exp2((folded - peak) * SCORE_SCALE)
    total = jnp.sum(exps, axis=2, keepdims=True)
    probs = jnp.concatenate([jnp.where(current, 0.0, exps), jnp.where(current, exps, 0.0)], axis=2).astype(BF16)
    raw = nn(probs.reshape(n * TILE, 2 * TILE), v).reshape(n, TILE, DH)
    inverse = 1.0 / total
    mean_square = jnp.mean(raw * raw, axis=2, keepdims=True) * (inverse * inverse)
    return raw * (inverse * lax.rsqrt(mean_square + EPSILON))


def partner_of(shard, stage):
    unit = 4 ** (stage // 2)
    digit = shard // unit % 4
    other = 3 - digit if stage % 2 else digit + 1 - 2 * (digit % 2)
    return shard + (other - digit) * unit


def kernel(
    table_hbm,
    lengths_hbm,
    index_hbm,
    gain_lin_hbm,
    gain_win_hbm,
    q_hbm,
    k_hbm,
    v_hbm,
    wk_hbm,
    wv_hbm,
    w_hbm,
    own_ref,
    other_ref,
    table_ref,
    lengths_ref,
    index_ref,
    gain_lin_ref,
    gain_win_ref,
    q_ref,
    k_ref,
    v_ref,
    qt_ref,
    vt_ref,
    window_ref,
    wkt_ref,
    rim_ref,
    w_ref,
    weights_ref,
    tile_ref,
    run_ref,
    send_ref,
    recv_ref,
    lin_ref,
    win_ref,
    att_ref,
    part_ref,
    small_sem,
    kv_sem,
    q_sem,
    win_sem,
    w_sem,
    send_sem,
    recv_sem,
    rim_load_sem,
    rim_send_sem,
    rim_recv_sem,
    part_send_sem,
    part_recv_sem,
):
    heads, tokens, _ = q_ref.shape
    groups = window_ref.shape[1]
    members = heads // groups
    tiles = tokens // TILE
    stages = recv_ref.shape[1]
    own_rows = own_ref.shape[0]
    own_tiles = own_rows // TILE
    shard = lax.axis_index("seq")
    core = lax.axis_index("head")

    def columns(hbm, h):
        return hbm.at[:, pl.ds(pl.multiple_of(h * DH, DH), DH)]

    def k_copy(h):
        return pltpu.make_async_copy(columns(k_hbm, h), k_ref.at[h], kv_sem.at[0, h])

    def v_copy(h):
        return pltpu.make_async_copy(columns(v_hbm, h), v_ref.at[h], kv_sem.at[1, h])

    def q_copy(h):
        return pltpu.make_async_copy(columns(q_hbm, h), q_ref.at[h], q_sem.at[h])

    def wk_copy(g):
        return pltpu.make_async_copy(columns(wk_hbm, g), window_ref.at[0, g, pl.ds(TILE, tokens)], win_sem.at[0, g])

    def wv_copy(g):
        return pltpu.make_async_copy(columns(wv_hbm, g), window_ref.at[1, g, pl.ds(TILE, tokens)], win_sem.at[1, g])

    w_copy = pltpu.make_async_copy(w_hbm, w_ref, w_sem)

    def hop(stage, h):
        return pltpu.make_async_remote_copy(
            src_ref=send_ref.at[stage, h],
            dst_ref=recv_ref.at[h, stage],
            send_sem=send_sem.at[stage, h],
            recv_sem=recv_sem.at[stage, h],
            device_id={"seq": partner_of(shard, stage)},
            device_id_type=MESH,
        )

    place = [shard % 4, shard // 4 % 4, shard // 16]
    rim_count = groups * RIM_PIECES
    last_y = place[0] == 3
    on_leg = [last_y, jnp.logical_and(last_y, place[1] == 0), place[0] >= 0]
    from_z = jnp.logical_and(last_y, place[1] > 0)
    rim_slot = jnp.where(on_leg[1], 2, jnp.where(last_y, 1, 0))

    def rim(leg, n):
        rows = TILE // RIM_PIECES
        g, piece = n // RIM_PIECES, n % RIM_PIECES
        span = pl.ds(pl.multiple_of(piece * rows, rows), rows)
        axis = (1, 2, 0)[leg]
        return pltpu.make_async_remote_copy(
            src_ref=rim_ref.at[(0, 1, rim_slot)[leg], :, g, span],
            dst_ref=rim_ref.at[leg + 1, :, g, span],
            send_sem=rim_send_sem.at[leg, n],
            recv_sem=rim_recv_sem.at[leg, n],
            device_id={"seq": shard + ((place[axis] + 1) % 4 - place[axis]) * 4**axis},
            device_id_type=MESH,
        )

    def rim_load(which, g):
        hbm = (wk_hbm, wv_hbm)[which]
        return pltpu.make_async_copy(
            hbm.at[pl.ds(tokens - TILE, TILE), pl.ds(g * DH, DH)], rim_ref.at[0, which, g], rim_load_sem.at[which, g]
        )

    def part_copy(r):
        return pltpu.make_async_remote_copy(
            src_ref=part_ref.at[r],
            dst_ref=other_ref.at[pl.ds(r * TILE, TILE)],
            send_sem=part_send_sem.at[r],
            recv_sem=part_recv_sem.at[r],
            device_id={"head": 1 - core},
            device_id_type=MESH,
        )

    small = [
        pltpu.make_async_copy(hbm, ref, small_sem.at[n])
        for n, (hbm, ref) in enumerate(
            (
                (lengths_hbm, lengths_ref),
                (table_hbm, table_ref),
                (index_hbm, index_ref),
                (gain_lin_hbm, gain_lin_ref),
                (gain_win_hbm, gain_win_ref),
            )
        )
    ]
    for h in range(heads):
        k_copy(h).start()
        v_copy(h).start()
    for copy in small:
        copy.start()
    for g in range(groups):
        for which in range(2):
            rim_load(which, g).start()
    for h in range(heads):
        q_copy(h).start()
    for g in range(groups):
        wk_copy(g).start()
        wv_copy(g).start()
    w_copy.start()

    barrier = pltpu.get_barrier_semaphore()
    for stage in range(stages):
        pl.semaphore_signal(barrier, inc=1, device_id={"seq": partner_of(shard, stage)}, device_id_type=MESH)
    pl.semaphore_signal(barrier, inc=1, device_id={"head": 1 - core}, device_id_type=MESH)

    def state(h):
        k_copy(h).wait()
        v_copy(h).wait()
        vt_ref[h] = v_ref[h].T
        states = [
            nn(vt_ref[h, :, t * TILE : (t + 1) * TILE], k_ref[h, t * TILE : (t + 1) * TILE, :]) for t in range(tiles)
        ]
        pair = states[0] + states[1]
        tile_ref[h, 0] = states[0].astype(BF16)
        tile_ref[h, 1] = states[2].astype(BF16)
        tile_ref[h, 2] = pair.astype(BF16)
        total = pair + (states[2] + states[3])
        run_ref[h] = total
        send_ref[0, h] = total.astype(BF16)

    state(0)
    pl.semaphore_wait(barrier, stages + 1)
    hop(0, 0).start()

    @pl.loop(1, heads)
    def _(h):
        state(h)
        hop(0, h).start()

    for g in range(groups):
        for which in range(2):
            rim_load(which, g).wait()

    @pl.when(on_leg[0])
    def _():
        @pl.loop(0, rim_count)
        def _(n):
            rim(0, n).start()

    for copy in small:
        copy.wait()

    starts, begin, running_start = [], 0, 0
    for i in range(lengths_ref.shape[0]):
        starts.append(running_start)
        running_start = running_start + lengths_ref[i]
    for start in starts[1:]:
        begin = jnp.where(start <= shard, start, begin)
    opens_here = begin == shard

    def opened(base, span):
        found = False
        for start in starts:
            found = jnp.logical_or(found, jnp.logical_and(start >= base, start < base + span))
        return found

    keep, own_scale, partner_scale = [], [], []
    for stage in range(stages):
        span = 1 << stage
        base = shard // span * span
        upper = (shard // span) % 2 == 1
        other = jnp.where(upper, base - span, base + span)
        keep.append(jnp.where(jnp.logical_and(upper, begin < base), 1.0, 0.0))
        own_scale.append(jnp.where(jnp.logical_and(jnp.logical_not(upper), opened(other, span)), 0.0, 1.0))
        partner_scale.append(jnp.where(jnp.logical_and(upper, opened(base, span)), 0.0, 1.0))

    @pl.loop(0, heads)
    def _(h):
        weights_ref[h] = head_weights(index_ref[...], table_ref, h)

    def tick(n):
        for stage in range(stages - 1):
            h = n - LAG * stage

            @pl.when(jnp.logical_and(h >= 0, h < heads))
            def _():
                hop(stage, h).wait_recv()
                total = own_scale[stage] * run_ref[h] + partner_scale[stage] * recv_ref[h, stage].astype(F32)
                run_ref[h] = total
                send_ref[stage + 1, h] = total.astype(BF16)
                hop(stage + 1, h).start()

        piece = n - RIM_X

        @pl.when(jnp.logical_and(on_leg[1], jnp.logical_and(piece >= 0, piece < rim_count)))
        def _():
            rim(0, piece).wait_recv()
            rim(1, piece).start()

        last = n - RIM_Y

        @pl.when(jnp.logical_and(last >= 0, last < rim_count))
        def _():
            @pl.when(from_z)
            def _():
                rim(0, last).wait_recv()

            @pl.when(on_leg[1])
            def _():
                rim(1, last).wait_recv()

            rim(2, last).start()

    for g in range(groups):
        wk_copy(g).wait()
        wv_copy(g).wait()
        for tile in range(1, tiles + 1):
            wkt_ref[g, tile] = window_ref[0, g, tile * TILE : (tile + 1) * TILE, :].T

    pattern = level_pattern(TILE // 2)
    t = lax.broadcasted_iota(jnp.int32, (TILE, TILE), 0)
    s = lax.broadcasted_iota(jnp.int32, (TILE, TILE), 1)
    current = s <= t

    def near(h, tile):
        first = tile * TILE
        qt = qt_ref[h, :, first : first + TILE]

        def rows(level):
            return weights_ref[h, level : level + 1, first : first + TILE]

        total = near_tile(qt, k_ref[h, first : first + TILE, :], vt_ref[h, :, first : first + TILE], rows, pattern)
        if tile % 2:
            total = total + rows(9) * nn(tile_ref[h, tile // 2], qt)
        if tile >= 2:
            total = total + rows(10) * nn(tile_ref[h, 2], qt)
        lin_ref[h, :, first : first + TILE] = total

    def window(g, tile, penalty):
        first = tile * TILE if isinstance(tile, int) else pl.multiple_of(tile * TILE, TILE)
        mine = pl.ds(g * members, members)
        raw = window_rows(
            q_ref[mine, pl.ds(first, TILE), :],
            jnp.concatenate([wkt_ref[g, tile], wkt_ref[g, tile + 1]], axis=1),
            window_ref[1, g, pl.ds(first, 2 * TILE), :],
            current,
            penalty,
        )
        win_ref[mine, pl.ds(first, TILE), :] = raw * gain_win_ref[mine]

    def far(h, tile, first_stage, last_stage):
        first = tile * TILE
        qt = qt_ref[h, :, first : first + TILE]
        count = last_stage - first_stage
        reached = nn(recv_ref[h, first_stage:last_stage].reshape(count * DH, DH), qt)
        lin = lin_ref[h, :, first : first + TILE]
        for i in range(count):
            level = 11 + first_stage + i
            row = weights_ref[h, level : level + 1, first : first + TILE] * keep[first_stage + i]
            lin = lin + row * reached[i * DH : (i + 1) * DH]
        return lin

    for h in range(heads):
        q_copy(h).wait()

    @pl.loop(0, heads)
    def _(i):
        qt_ref[i] = q_ref[i].T
        near(i, 0)
        near(i, 1)
        tick(3 * i)

        near(i, 2)
        near(i, 3)
        tick(3 * i + 1)

        @pl.when(i < groups * (tiles - 1))
        def _():
            window(i % groups, 1 + i // groups, None)

        tick(3 * i + 2)

    early = stages - 2

    @pl.loop(0, heads)
    def _(h):
        for tile in range(tiles):
            lin_ref[h, :, tile * TILE : (tile + 1) * TILE] = far(h, tile, 0, early)
        tick(3 * heads + h)

    @pl.loop(0, rim_count)
    def _(n):
        rim(2, n).wait_recv()

    for g in range(groups):
        wkt_ref[g, 0] = rim_ref[3, 0, g].T
        window_ref[1, g, :TILE, :] = rim_ref[3, 1, g]
        window(g, 0, jnp.where(opens_here, -1e30, 0.0))

    @pl.loop(0, heads)
    def _(h):
        hop(stages - 1, h).wait_recv()
        for tile in range(tiles):
            span = pl.ds(tile * TILE, TILE)
            lin = far(h, tile, early, stages)
            mean_square = jnp.mean(lin * lin, axis=0, keepdims=True)
            lin = (lin * lax.rsqrt(mean_square + EPSILON)).T * gain_lin_ref[h]
            att_ref[span, pl.ds(pl.multiple_of(h * DH, DH), DH)] = (lin + win_ref[h, span, :]).astype(BF16)

    w_copy.wait()

    def project(owner, r):
        first = pl.multiple_of(owner * own_rows + r * TILE, TILE)
        return nn(att_ref[pl.ds(first, TILE), :], w_ref[...]).astype(BF16)

    @pl.loop(0, own_tiles)
    def _(r):
        part_ref[r] = project(1 - core, r)
        part_copy(r).start()

    @pl.loop(0, own_tiles)
    def _(r):
        own_ref[pl.ds(pl.multiple_of(r * TILE, TILE), TILE), :] = project(core, r)

    for leg in range(3):

        @pl.when(on_leg[leg])
        def _():
            @pl.loop(0, rim_count)
            def _(n):
                rim(leg, n).wait_send()

    @pl.loop(0, heads)
    def _(h):
        for stage in range(stages):
            hop(stage, h).wait_send()

    for r in range(own_tiles):
        part_copy(r).wait()


def shards(
    queries,
    lin_keys,
    lin_values,
    window_keys,
    window_values,
    level_index,
    level_table,
    seq_lengths,
    gain_linear,
    gain_window,
    w_out,
):
    tokens = queries.shape[0]
    heads = level_table.shape[1]
    groups = window_keys.shape[1] // DH
    levels = level_index.shape[0]
    tiles = tokens // TILE
    stages = lax.axis_size("seq").bit_length() - 1
    width = w_out.shape[1]
    own_rows = tokens // lax.axis_size("head")
    own_tiles = own_rows // TILE
    vmem = pl.BlockSpec(memory_space=pltpu.VMEM)
    hbm = pl.BlockSpec(memory_space=pltpu.HBM)
    dma = pltpu.SemaphoreType.DMA
    own, other = pl.pallas_call(
        kernel,
        in_specs=[hbm] * 11,
        out_specs=[vmem] * 2,
        out_shape=[pltpu.VMEM((own_rows, width), BF16)] * 2,
        scratch_shapes=[
            pltpu.SMEM(level_table.shape, F32),
            pltpu.SMEM(seq_lengths.shape, jnp.int32),
            pltpu.VMEM(level_index.shape, jnp.int32),
            pltpu.VMEM((heads, 1, DH), F32),
            pltpu.VMEM((heads, 1, DH), F32),
            pltpu.VMEM((heads, tokens, DH), BF16),
            pltpu.VMEM((heads, tokens, DH), BF16),
            pltpu.VMEM((heads, tokens, DH), BF16),
            pltpu.VMEM((heads, DH, tokens), BF16),
            pltpu.VMEM((heads, DH, tokens), BF16),
            pltpu.VMEM((2, groups, TILE + tokens, DH), BF16),
            pltpu.VMEM((groups, tiles + 1, DH, TILE), BF16),
            pltpu.VMEM((4, 2, groups, TILE, DH), BF16),
            pltpu.VMEM(w_out.shape, BF16),
            pltpu.VMEM((heads, levels, tokens), F32),
            pltpu.VMEM((heads, 3, DH, DH), BF16),
            pltpu.VMEM((heads, DH, DH), F32),
            pltpu.VMEM((stages, heads, DH, DH), BF16),
            pltpu.VMEM((heads, stages, DH, DH), BF16),
            pltpu.VMEM((heads, DH, tokens), F32),
            pltpu.VMEM((heads, tokens, DH), F32),
            pltpu.VMEM((tokens, heads * DH), BF16),
            pltpu.VMEM((own_tiles, TILE, width), BF16),
            dma((5,)),
            dma((2, heads)),
            dma((heads,)),
            dma((2, groups)),
            dma,
            dma((stages, heads)),
            dma((stages, heads)),
            dma((2, groups)),
            dma((3, groups * RIM_PIECES)),
            dma((3, groups * RIM_PIECES)),
            dma((own_tiles,)),
            dma((own_tiles,)),
        ],
        compiler_params=pltpu.CompilerParams(
            collective_id=0, has_side_effects=True, vmem_limit_bytes=48 << 20
        ),
    )(
        *(
            pltpu.with_memory_space_constraint(x, pltpu.HBM)
            for x in (
                level_table,
                seq_lengths,
                level_index,
                gain_linear.reshape(heads, 1, DH),
                gain_window.reshape(heads, 1, DH),
                queries,
                lin_keys,
                lin_values,
                window_keys,
                window_values,
                w_out,
            )
        )
    )
    return (own.astype(F32) + other.astype(F32)).astype(BF16)


def solution(mesh):
    placed = (
        P("seq", "head"),
        P("seq", "head"),
        P("seq", "head"),
        P("seq", "head"),
        P("seq", "head"),
        P(None, "seq"),
        P(None, "head"),
        P(),
        P("head"),
        P("head"),
        P("head", None),
    )
    return jax.shard_map(
        shards, mesh=mesh, in_specs=placed, out_specs=P(("seq", "head"), None), check_vma=False
    )
```
